256 devices in a mesh: ctx: 32 (over y, z_lo, core), ch: 8 (over z_hi, x).
Axes of the slice: x: 4, y: 4, z: 8 (z_hi: 2, z_lo: 4; z = z_hi * 4 + z_lo), core: 2. Of those that a mesh axis runs over, the one named last changes fastest.
Arguments:
- token_ids: int32 [16384], P('ctx'), may hold values from 65 to 84, as said below
- embedding: bfloat16 [512, 4096], P(None, 'ch'), may hold values from -6 to 6
- long_table: bfloat16 [512, 3, 4096], P(None, None, 'ch'), may hold values from -6 to 6
- long_taps: float32 [3, 3, 4096], P(None, None, 'ch'), may hold values from -3 to 3
- long_residue: float32 [256, 16], P('ch'), may hold values from -1.5 to 1.5
- long_rate: float32 [256, 16], P('ch'), may hold values from 1.2207031e-06 to 0.04
- long_skip: float32 [4096], P('ch'), may hold values from 0.25 to 1.75
- medium_gain: bfloat16 [4096], P('ch'), may hold values from 0.25 to 1.75
- medium_weight: bfloat16 [4096, 3, 4096], P('ctx', None, 'ch'), may hold values from -0.09375 to 0.09375
- medium_taps: float32 [3, 3, 4096], P(None, None, 'ch'), may hold values from -3 to 3
- medium_group_filter: float32 [256, 128], P('ch'), may hold values from -0.6 to 0.6
- medium_skip: float32 [4096], P('ch'), may hold values from 0.25 to 1.75
- filter_group: int32 [4096], P('ch'), may hold values from 0 to 255, as said below
Outputs:
- block_output: bfloat16 [16384, 4096], P('ctx', 'ch')
The draws below stay inside these ranges and needn't reach their ends.
Inputs may be any that keep to these rules, and one draw needn't show every extreme that they name: `token_ids`: every token is the byte code of A, C, G, T or N. `filter_group`: each filter group has exactly 16 channels, all within one block of 512 consecutive channels; block j holds groups j * (32) to (j + 1) * 32 - 1.
All inputs are finite; a program needn't handle non-finite values.
Results may differ from the reference program's by a relative error of at most 0.006.
Values may be sent and summed in bfloat16 or wider, within the bound.
A program may use at most 128 MiB of HBM per device.

```python
import math
import jax
import jax.numpy as jnp
from jax import lax

MODEL_WIDTH = 4096
V = 512
GS = 16
P_SIZE = 16
MEDIUM_TAPS = 128
WINDOW_TOKENS = 16384
FILTER_GROUPS = 256
DPD = 512


def draw_token_ids(key, part):
    codes = jnp.array([65, 67, 71, 84, 78], jnp.int32)
    choice_index = jax.random.randint(jax.random.fold_in(key, 11), (WINDOW_TOKENS,), 0, 5)
    return jnp.take(codes, choice_index)


def draw_filter_group(key, part):
    blocks = MODEL_WIDTH // DPD
    keys = jax.random.split(jax.random.fold_in(key, 23), blocks)
    orders = jax.vmap(lambda single: jax.random.permutation(single, DPD))(keys)
    offsets = (jnp.arange(blocks, dtype=jnp.int32) * (DPD // GS))[:, None]
    return (orders.astype(jnp.int32) // GS + offsets).reshape(MODEL_WIDTH).astype(jnp.int32)


def block_scale(rng, dims, cuts, smallest, high):
    def one(axis_at, shards_of):
        heights = jax.random.uniform(jax.random.fold_in(jax.random.fold_in(rng, 6), axis_at), (shards_of,), jnp.float32, smallest / len(cuts), high / len(cuts))
        return jnp.repeat(jnp.exp(heights), dims[axis_at] // shards_of).reshape((-1,) + (1,) * (len(dims) - axis_at - 1))

    level = one(*cuts[0])
    for cut in cuts[1:]:
        level = level * one(*cut)
    return level


def centred(key, dims, scale, bound, cuts=(), held_as=jnp.bfloat16):
    loudness = block_scale(key, dims, cuts, -0.22, 0.18) if cuts else 1.0
    entries = jax.random.normal(key, dims, jnp.float32) * scale * loudness
    return jnp.minimum(jnp.maximum(entries, -bound), bound).astype(held_as)


def setup_inputs(seed: int = 0) -> dict:
    splits = jax.random.split(jax.random.key(seed), 14)
    token_ids = draw_token_ids(jax.random.fold_in(splits[13], 71), 0)
    embedding = centred(splits[1], (V, MODEL_WIDTH), 1.0, 6.0, ((1, 8),))
    long_table = centred(splits[2], (V, 3, MODEL_WIDTH), 1.0, 6.0, ((2, 8),))
    long_taps = centred(splits[3], (3, 3, MODEL_WIDTH), 0.6, 3.0, ((2, 8),), jnp.float32)
    long_residue = centred(splits[4], (FILTER_GROUPS, P_SIZE), 0.25, 1.5, ((0, 8),), jnp.float32)
    long_rate = jnp.clip(jnp.exp(math.log(0.04) - 10.3972077 * jax.random.uniform(splits[5], (FILTER_GROUPS, P_SIZE), jnp.float32) ** block_scale(splits[5], (FILTER_GROUPS, P_SIZE), ((0, 8),), -0.2, 0.2)), 1.220703097715159e-06, 0.04)
    long_skip = jnp.clip(1.0 + 0.15 * jax.random.normal(splits[6], (MODEL_WIDTH,), jnp.float32), 0.25, 1.75)
    medium_gain = jnp.clip(1.0 + 0.15 * jax.random.normal(splits[7], (MODEL_WIDTH,), jnp.float32), 0.25, 1.75).astype(jnp.bfloat16)
    medium_weight = centred(splits[8], (MODEL_WIDTH, 3, MODEL_WIDTH), MODEL_WIDTH ** -0.5, 0.09375, ((0, 32), (2, 8)))
    medium_taps = centred(splits[9], (3, 3, MODEL_WIDTH), 0.6, 3.0, ((2, 8),), jnp.float32)
    medium_group_filter = centred(splits[10], (FILTER_GROUPS, MEDIUM_TAPS), (MEDIUM_TAPS ** -0.5), 0.6, ((0, 8),), jnp.float32)
    medium_skip = jnp.clip(1.0 + 0.15 * jax.random.normal(splits[11], (MODEL_WIDTH,), jnp.float32), 0.25, 1.75)
    filter_group = draw_filter_group(jax.random.fold_in(splits[13], 71), 0)
    return dict(token_ids=token_ids, embedding=embedding, long_table=long_table, long_taps=long_taps, long_residue=long_residue, long_rate=long_rate, long_skip=long_skip, medium_gain=medium_gain, medium_weight=medium_weight, medium_taps=medium_taps, medium_group_filter=medium_group_filter, medium_skip=medium_skip, filter_group=filter_group)


epsilon = 1e-06

def featurize(streams, filter_taps):
    wide = streams.astype(jnp.float32)
    length = wide.shape[0]
    padded_input = jnp.concatenate([jnp.zeros((2,) + wide.shape[1:], jnp.float32), wide], axis=0)
    mixed = filter_taps[0] * padded_input[2:2 + length]
    mixed = mixed + filter_taps[1] * padded_input[1:1 + length]
    mixed = mixed + filter_taps[2] * padded_input[0:length]
    return mixed

def reference(token_ids, embedding, long_table, long_taps, long_residue, long_rate, long_skip, medium_gain, medium_weight, medium_taps, medium_group_filter, medium_skip, filter_group):
    resid = jnp.take(embedding, token_ids, axis=0)
    streams = jnp.take(long_table, token_ids, axis=0)
    mixed = featurize(streams, long_taps)
    query = mixed[:, 0]
    product = (mixed[:, 1] * mixed[:, 2]).astype(jnp.bfloat16)
    product_wide = product.astype(jnp.float32)
    rate_chan = jnp.take(long_rate, filter_group, axis=0)
    residue_chan = jnp.take(long_residue, filter_group, axis=0)
    decay = jnp.exp(-rate_chan)
    weight_res = residue_chan * jnp.sqrt(-jnp.expm1(-2.0 * rate_chan))

    def advance(state, row):
        state = decay * state + row[:, None]
        return (state, lax.optimization_barrier(jnp.sum(weight_res * state, axis=1)))
    initial = jnp.zeros((MODEL_WIDTH, P_SIZE), jnp.float32)
    _, conv_long = lax.scan(advance, initial, product_wide)
    conv_long = conv_long + long_skip * product_wide
    middle = (resid.astype(jnp.float32) + query * conv_long).astype(jnp.bfloat16)
    middle_wide = middle.astype(jnp.float32)
    scale = lax.rsqrt(lax.optimization_barrier(jnp.sum(middle_wide * middle_wide, axis=1, keepdims=True)) / MODEL_WIDTH + epsilon)
    normed = (middle_wide * scale * medium_gain.astype(jnp.float32)).astype(jnp.bfloat16)
    projected = jnp.dot(normed, medium_weight.reshape(MODEL_WIDTH, 3 * MODEL_WIDTH), preferred_element_type=jnp.float32)
    projected = projected.astype(jnp.bfloat16).reshape(WINDOW_TOKENS, 3, MODEL_WIDTH)
    mixed2 = featurize(projected, medium_taps)
    query2 = mixed2[:, 0]
    product2 = (mixed2[:, 1] * mixed2[:, 2]).astype(jnp.bfloat16)
    second_product_wide = product2.astype(jnp.float32)
    filter_chan = jnp.take(medium_group_filter, filter_group, axis=0)
    padded_input = jnp.concatenate([jnp.zeros((MEDIUM_TAPS - 1, MODEL_WIDTH), jnp.float32), second_product_wide], axis=0)

    def accumulate_tap(tap_delay, total):
        column = lax.dynamic_index_in_dim(filter_chan, tap_delay, 1, keepdims=False)
        genome_window = lax.dynamic_slice_in_dim(padded_input, MEDIUM_TAPS - 1 - tap_delay, WINDOW_TOKENS, 0)
        return total + column * genome_window
    medium_convolution = lax.fori_loop(0, MEDIUM_TAPS, accumulate_tap, jnp.zeros((WINDOW_TOKENS, MODEL_WIDTH), jnp.float32))
    medium_convolution = medium_convolution + medium_skip * second_product_wide
    return (middle_wide + query2 * medium_convolution).astype(jnp.bfloat16)
```

```python
import functools

import jax
import jax.numpy as jnp
from jax import lax
from jax.experimental import pallas as pl
from jax.experimental.pallas import tpu as pltpu
from jax.sharding import PartitionSpec as P

EPSILON = 1e-06
HALO = 144
F32 = jnp.float32
BF16 = jnp.bfloat16


def kernel(
    sizes,
    token_ref,
    emb_ref,
    table_ref,
    ltaps_ref,
    residue_ref,
    rate_ref,
    lskip_ref,
    gain_ref,
    w_ref,
    mtaps_ref,
    filt_ref,
    mskip_ref,
    group_ref,
    out_ref,
    emb,
    table,
    tok_ref,
    weights,
    feats,
    acc,
    hot,
    halo_tok,
    prod,
    query,
    resid,
    conv,
    chan,
    excl,
    end_own,
    end_other,
    chip_own,
    chip_all,
    row_own,
    row_all,
    note_own,
    note_all,
    scale,
    half_norm,
    perm,
    toep,
    tail_out,
    tail_in,
    prod2,
    turned,
    conv_hi,
    conv_lo,
    load_sem,
    tok_sem,
    z_sem,
    y_sem,
    pair_sem,
    end_sem,
    chip_sem,
    row_sem,
    note_sem,
    x_sem,
    far_sem,
    tail_sem,
):
    ny, nz, nh, nx = sizes
    nch = nh * nx
    tokens, width = query.shape
    piece = w_ref.shape[1]
    ctx, ch = lax.axis_index("ctx"), lax.axis_index("ch")
    core, chip = ctx % 2, ctx // 2
    z, y = chip % nz, chip // nz
    x, h = ch % nx, ch // nx
    last_ctx = 2 * ny * nz - 1
    waits = []

    def along(yy, zz, cc):
        return {"ctx": (yy * nz + zz) * 2 + cc}

    def across(hh, xx):
        return {"ch": hh * nx + xx}

    def copy(src, dst, sems, to):
        made = pltpu.make_async_remote_copy(
            src_ref=src,
            dst_ref=dst,
            send_sem=sems[0],
            recv_sem=sems[1],
            device_id=to,
            device_id_type=pl.DeviceIdType.MESH,
        )
        return made

    def send(make, cond=None):
        copy(*make()).start()
        waits.append((make, cond))

    def sems_of(ref, *index):
        return ref.at[(0, *index)], ref.at[(1, *index)]

    def arrived(dst, sems, to):
        copy(dst, dst, sems, to).wait_recv()

    barrier = pltpu.get_barrier_semaphore()
    peers = [along(y, z, 1 - core)]
    peers += [along(y, (z + o) % nz, core) for o in range(1, nz)]
    peers += [along((y + o) % ny, z, core) for o in range(1, ny)]
    peers += [{"ch": (ch + o) % nch} for o in range(1, nch)]
    for peer in peers:
        pl.semaphore_signal(barrier, inc=1, device_id=peer, device_id_type=pl.DeviceIdType.MESH)
    has_next = jnp.logical_and(core == 1, ctx < last_ctx)
    has_before = jnp.logical_and(core == 0, ctx > 0)

    @pl.when(has_next)
    def _():
        pl.semaphore_signal(
            barrier, inc=1, device_id={"ctx": ctx + 1}, device_id_type=pl.DeviceIdType.MESH
        )

    @pl.when(has_before)
    def _():
        pl.semaphore_signal(
            barrier, inc=1, device_id={"ctx": ctx - 1}, device_id_type=pl.DeviceIdType.MESH
        )

    def rows_of(slot):
        return pl.ds(pl.multiple_of(slot * piece, piece), piece)

    def part_of(slot, part):
        return pl.ds(pl.multiple_of(slot * piece + part * (piece // 2), piece // 2), piece // 2)

    loads = [
        pltpu.make_async_copy(
            w_ref.at[i], weights.at[rows_of(ctx), pl.ds(i * width, width)], load_sem.at[i]
        )
        for i in range(3)
    ]
    loads.append(pltpu.make_async_copy(emb_ref.at[pl.ds(64, 32)], emb, load_sem.at[3]))
    loads.append(pltpu.make_async_copy(table_ref.at[:, pl.ds(64, 32)], table, load_sem.at[4]))
    for load in loads:
        load.start()
    tok_ref[...] = jnp.broadcast_to(token_ref[...], tok_ref.shape)

    def slot(yy, zz, cc):
        return (yy * nz + zz) * 2 + cc

    def event_of(e):
        if e == 0:
            return z, None
        r = (e - 1) // 2
        if e % 2 == 1:
            return z - 1 - r, lambda: z - 1 - r >= 0
        return z + 1 + r, lambda: z + 1 + r < nz

    def guarded(cond, body):
        if cond is None:
            body()
        else:
            pl.when(cond())(body)

    up, down = (y + 1) % ny, (y + ny - 1) % ny

    def pair(e, kind, rows, cond):
        def make():
            view = weights.at[rows()]
            return view, view, sems_of(pair_sem, e, kind), along(y, z, 1 - core)

        send(make, cond)

    def y_sends(e, zz, cond):
        if ny > 1:
            for way, to in ((0, up), (1, down)):

                def make(way=way, to=to):
                    view = weights.at[rows_of(slot(y, zz, core))]
                    return view, view, sems_of(y_sem, e, way), along(to, z, core)

                send(make, cond)

    def z_send(way, hop, zz, cond):
        def inside():
            return z + 1 < nz if way == 0 else z > 0

        def wanted():
            return inside() if cond is None else jnp.logical_and(cond(), inside())

        def make():
            view = weights.at[rows_of(slot(y, zz, core))]
            to = z + 1 if way == 0 else z - 1
            return view, view, sems_of(z_sem, hop, way), along(y, to, core)

        pl.when(inside())(lambda: send(make, wanted))

    def own_weights():
        if nz > 1:
            z_send(0, 0, z, None)
            z_send(1, 0, z, None)
        y_sends(0, z, None)
        pair(0, 0, lambda: rows_of(slot(y, z, core)), None)

    def z_forward(r):
        for way in (0, 1):
            e = 1 + 2 * r + way
            zz, valid = event_of(e)

            def body(way=way, e=e, zz=zz, valid=valid):
                rows = rows_of(slot(y, zz, core))
                arrived(
                    weights.at[rows],
                    (z_sem.at[0, r, way], z_sem.at[1, r, way]),
                    along(y, zz, core),
                )
                if r + 1 < nz - 1:
                    z_send(way, r + 1, zz, valid)

            guarded(valid, body)

    def z_spread(r):
        for way in (0, 1):
            e = 1 + 2 * r + way
            zz, valid = event_of(e)

            def body(e=e, zz=zz, valid=valid):
                y_sends(e, zz, valid)
                pair(e, 0, lambda: rows_of(slot(y, zz, core)), valid)

            guarded(valid, body)

    def z_round(r):
        z_forward(r)
        z_spread(r)

    def y_first(e):
        zz, valid = event_of(e)

        def body():
            for way, origin, to in ((0, down, up), (1, up, down)):
                rows = rows_of(slot(origin, zz, core))
                arrived(
                    weights.at[rows],
                    (y_sem.at[0, e, way], y_sem.at[1, e, way]),
                    along(origin, z, core),
                )

                def make(way=way, origin=origin, to=to):
                    view = weights.at[part_of(slot(origin, zz, core), way)]
                    return view, view, sems_of(y_sem, e, 2 + way), along(to, z, core)

                send(make, valid)
                pair(e, 1 + way, lambda origin=origin: rows_of(slot(origin, zz, core)), valid)

        if ny > 1:
            guarded(valid, body)

    def y_second(e):
        zz, valid = event_of(e)

        def body():
            for way, origin in ((0, down), (1, up)):
                half = part_of(slot((y + 2) % ny, zz, core), way)
                arrived(
                    weights.at[half],
                    (y_sem.at[0, e, 2 + way], y_sem.at[1, e, 2 + way]),
                    along(origin, z, core),
                )
                pair(
                    e, 3 + way, lambda way=way: part_of(slot((y + 2) % ny, zz, core), way), valid
                )

        if ny > 1:
            guarded(valid, body)

    def pair_in(e, kinds):
        zz, valid = event_of(e)

        def body():
            other = along(y, z, 1 - core)

            def one(kind, rows):
                if kind in kinds:
                    arrived(weights.at[rows], sems_of(pair_sem, e, kind), other)

            one(0, rows_of(slot(y, zz, 1 - core)))
            if ny > 1:
                one(1, rows_of(slot(down, zz, 1 - core)))
                one(2, rows_of(slot(up, zz, 1 - core)))
                one(3, part_of(slot((y + 2) % ny, zz, 1 - core), 0))
                one(4, part_of(slot((y + 2) % ny, zz, 1 - core), 1))

        guarded(valid, body)

    events = list(range(1 + 2 * (nz - 1)))

    group_row = (group_ref[...] - ch * (width // 16)).astype(F32)
    of_group = (
        lax.broadcasted_iota(jnp.int32, (32, width), 0).astype(F32) == group_row
    ).astype(F32)
    rate_in = rate_ref[...]
    twice = 2.0 * rate_in
    series = jnp.ones_like(twice)
    for k in range(9, 1, -1):
        series = 1.0 - twice * (1.0 / k) * series
    both = jnp.concatenate([rate_in, residue_ref[...] * jnp.sqrt(twice * series)], axis=0)
    chan[...] = jnp.dot(
        both, of_group, precision=lax.Precision.HIGHEST, preferred_element_type=F32
    )

    def one_hots(joined, count):
        codes = 64 + lax.broadcasted_iota(jnp.int32, (32, count), 0)
        for back in range(3):
            shifted = joined if back == 0 else pltpu.roll(joined, back, 1)
            row = shifted[0:1, 128:]
            hot[back, 0:count] = (row == codes).astype(F32).T.astype(BF16)

    def streams(rows):
        for tile in range(width // 128):
            cols = pl.ds(tile * 128, 128)

            def mixed(i, cols=cols):
                total = None
                for back in range(3):
                    picked = jnp.dot(
                        hot[back, 0:rows], table[i, :, cols], preferred_element_type=F32
                    )
                    term = ltaps_ref[back, i : i + 1, cols] * picked
                    total = term if total is None else total + term
                return total

            key = mixed(1)
            prod[tile, 0:rows] = (key * mixed(2)).astype(BF16).astype(F32)
            query[0:rows, cols] = mixed(0)

    one_hots(jnp.concatenate([jnp.full((8, 128), -1, jnp.int32), tok_ref[...]], axis=1), tokens)
    loads[3].wait()
    loads[4].wait()
    resid[...] = jnp.dot(hot[0], emb[...], preferred_element_type=F32)
    streams(tokens)

    extra = jnp.logical_or(has_next, has_before)
    pl.semaphore_wait(barrier, len(peers) + extra.astype(jnp.int32))
    tail_tok = pl.ds(tokens - 128, 128)

    @pl.when(ctx < last_ctx)
    def _():
        send(
            lambda: (tok_ref.at[:, tail_tok], halo_tok, sems_of(tok_sem), {"ctx": ctx + 1}),
            lambda: ctx < last_ctx,
        )

    for load in loads[:3]:
        load.wait()
    own_weights()

    taps = filt_ref.shape[1]

    def make_toep(g, carry):
        line = filt_ref[pl.ds(g, 1), :]
        line = jnp.concatenate([line, jnp.zeros((1, taps), F32)], axis=1)
        spread = jnp.broadcast_to(line, (2 * taps, 2 * taps))
        turned_line = pltpu.roll(spread, taps, 1, stride=1, stride_axis=0)
        toep[g] = turned_line[:, :taps].astype(BF16)
        return carry

    lax.fori_loop(0, filt_ref.shape[0], make_toep, 0)
    lanes = lax.broadcasted_iota(jnp.int32, (128, width), 1)
    rank = jnp.zeros((1, width), F32)
    group_col = jnp.broadcast_to(group_row, (128, width)).T
    for tile in range(width // 128):
        mine = group_col[tile * 128 : (tile + 1) * 128, 0:1]
        above = tile * 128 + lax.broadcasted_iota(jnp.int32, (128, width), 0) < lanes
        same = jnp.logical_and(mine == group_row, above)
        rank = rank + jnp.sum(same.astype(F32), axis=0, keepdims=True)
    placed = group_row * float(width // 32) + rank
    for tile in range(width // 128):
        place = (tile * 128 + lax.broadcasted_iota(jnp.int32, (128, width), 0)).astype(F32)
        perm[tile * 128 : (tile + 1) * 128, :] = (place == placed).astype(F32).astype(BF16)

    @pl.when(ctx > 0)
    def _():
        arrived(halo_tok, (tok_sem.at[0], tok_sem.at[1]), {"ctx": ctx - 1})
        one_hots(jnp.concatenate([halo_tok[...], tok_ref[:, 0:128]], axis=1), 128)
        streams(16)

    chunk = tokens // 8
    chunk_id = lax.broadcasted_iota(jnp.int32, (8, 128), 0)

    def row_b(ref, p, cols):
        return jnp.broadcast_to(ref[p : p + 1, cols], (8, 128))

    for tile in range(width // 128):
        cols = pl.ds(tile * 128, 128)
        decay = [jnp.exp(-row_b(chan, p, cols)) for p in range(16)]

        def step(k, states, tile=tile, decay=decay):
            row = prod[tile, pl.ds(k, 8, stride=chunk), :]
            return tuple(d * s + row for d, s in zip(decay, states))

        states = lax.fori_loop(
            0, chunk, step, tuple(jnp.zeros((8, 128), F32) for _ in range(16)), unroll=4
        )
        for p in range(16):
            rate = row_b(chan, p, cols) * float(chunk)
            total = states[p]
            for by in (1, 2, 4):
                moved = jnp.exp(-rate * float(by)) * pltpu.roll(total, by, 0)
                total = total + jnp.where(chunk_id >= by, moved, 0.0)
            end_own[p : p + 1, cols] = total[7:8]
            excl[p, :, cols] = jnp.where(chunk_id >= 1, pltpu.roll(total, 1, 0), 0.0)

    rates = chan[0:16, :]
    send(lambda: (end_own, end_other, sems_of(end_sem), along(y, z, 1 - core)))
    arrived(end_other, (end_sem.at[0], end_sem.at[1]), along(y, z, 1 - core))
    first = jnp.where(core == 0, end_own[...], end_other[...])
    second = jnp.where(core == 0, end_other[...], end_own[...])
    decay_dev = jnp.exp(-rates * float(tokens))
    chip_own[...] = first * decay_dev + second
    for o in range(1, nz):
        send(
            lambda o=o: (
                chip_own,
                chip_all.at[z],
                (chip_sem.at[0, (z + o) % nz], chip_sem.at[1, z]),
                along(y, (z + o) % nz, core),
            )
        )
    if nz > 1:
        z_forward(0)
    y_first(0)
    for o in range(1, nz):
        origin = (z + nz - o) % nz
        arrived(
            chip_all.at[origin], (chip_sem.at[0, z], chip_sem.at[1, origin]), along(y, origin, core)
        )
    decay_chip = jnp.exp(-rates * float(2 * tokens))
    whole = None
    for zz in range(nz):
        if nz == 1:
            this = chip_own[...]
        else:
            this = jnp.where(z == zz, chip_own[...], chip_all[zz])
        whole = this if whole is None else whole * decay_chip + this
    row_own[...] = whole
    for o in range(1, ny):

        @pl.when(y + o < ny)
        def _(o=o):
            send(
                lambda: (
                    row_own,
                    row_all.at[y],
                    (row_sem.at[0, (y + o) % ny], row_sem.at[1, y]),
                    along((y + o) % ny, z, core),
                ),
                lambda: y + o < ny,
            )

    if nz > 1:
        z_spread(0)
    for o in range(1, ny):

        @pl.when(y >= o)
        def _(o=o):
            origin = (y + ny - o) % ny
            arrived(
                row_all.at[origin],
                (row_sem.at[0, y], row_sem.at[1, origin]),
                along(origin, z, core),
            )

    decay_row = jnp.exp(-rates * float(2 * tokens * nz))
    carried = jnp.zeros((16, width), F32)
    for yy in range(ny - 1):
        carried = jnp.where(yy < y, carried * decay_row + row_all[yy], carried)
    for zz in range(nz - 1):
        carried = jnp.where(zz < z, carried * decay_chip + chip_all[zz], carried)
    carried = jnp.where(core == 1, carried * decay_dev + first, carried)
    end_other[...] = carried

    for tile in range(width // 128):
        cols = pl.ds(tile * 128, 128)
        start = []
        for p in range(16):
            rate = row_b(chan, p, cols) * float(chunk)
            start.append(
                excl[p, :, cols]
                + jnp.exp(-rate * chunk_id.astype(F32)) * row_b(end_other, p, cols)
            )
        decay = [jnp.exp(-row_b(chan, p, cols)) for p in range(16)]
        weigh = [row_b(chan, 16 + p, cols) for p in range(16)]

        def step2(k, states, tile=tile, decay=decay, weigh=weigh):
            where = pl.ds(k, 8, stride=chunk)
            row = prod[tile, where, :]
            states = tuple(d * s + row for d, s in zip(decay, states))
            sums = [None] * 4
            for p in range(16):
                term = weigh[p] * states[p]
                sums[p % 4] = term if sums[p % 4] is None else sums[p % 4] + term
            conv[tile, where, :] = (sums[0] + sums[1]) + (sums[2] + sums[3])
            return states

        lax.fori_loop(0, chunk, step2, tuple(start), unroll=2)

    squares = None
    for tile in range(width // 128):
        cols = pl.ds(tile * 128, 128)
        whole = conv[tile] + lskip_ref[:, cols] * prod[tile]
        middle = (resid[:, cols] + query[:, cols] * whole).astype(BF16)
        feats[ch, :, cols] = middle
        wide = middle.astype(F32)
        resid[:, cols] = wide
        squares = wide * wide if squares is None else squares + wide * wide
    note_own[...] = jnp.broadcast_to(jnp.sum(squares.T, axis=0, keepdims=True), note_own.shape)
    note_own[1:2, :] = gain_ref[...].astype(F32)
    for o in range(1, nch):
        send(
            lambda o=o: (
                note_own,
                note_all.at[ch],
                (note_sem.at[0, (ch + o) % nch], note_sem.at[1, ch]),
                {"ch": (ch + o) % nch},
            )
        )

    right, left = (x + 1) % nx, (x + nx - 1) % nx
    far_parts = 4
    far_rows = tokens // far_parts

    def rows_x(e):
        return (0, tokens) if e == 0 else ((e - 1) * far_rows, far_rows)

    def half_x(e, way):
        base, count = rows_x(e)
        return pl.ds(base + way * (count // 2), count // 2)

    def x_sends(e):
        if nx > 1:
            for way, to in ((0, right), (1, left)):

                def make(way=way, to=to):
                    view = feats.at[side(e) * nx + x, pl.ds(*rows_x(e))]
                    return view, view, sems_of(x_sem, e, way), across(h, to)

                send(make)

    def side(e):
        return h if e == 0 else 1 - h

    def x_first(e):
        if nx > 1:
            for way, origin, to in ((0, left, right), (1, right, left)):
                block = side(e) * nx + origin
                arrived(
                    feats.at[block, pl.ds(*rows_x(e))], sems_of(x_sem, e, way), across(h, origin)
                )

                def make(way=way, block=block, to=to):
                    part = feats.at[block, half_x(e, way)]
                    return part, part, sems_of(x_sem, e, 2 + way), across(h, to)

                send(make)

    def x_second(e):
        if nx > 1:
            for way, origin in ((0, left), (1, right)):
                part = feats.at[side(e) * nx + (x + 2) % nx, half_x(e, way)]
                arrived(part, sems_of(x_sem, e, 2 + way), across(h, origin))

    def far_in(k):
        if nh > 1:
            part = feats.at[(1 - h) * nx + x, pl.ds(k * far_rows, far_rows)]
            arrived(part, sems_of(far_sem, k), across(1 - h, x))
            x_sends(1 + k)

    def x_far_first(k):
        if nh > 1:
            x_first(1 + k)

    x_sends(0)
    if nz > 2:
        z_round(1)
    if nh > 1:
        for k in range(far_parts):

            def make(k=k):
                part = feats.at[ch, pl.ds(k * far_rows, far_rows)]
                return part, part, sems_of(far_sem, k), across(1 - h, x)

            send(make)

    def y_first_if(*which):
        for e in which:
            if e in events:
                y_first(e)

    def y_second_if(*which):
        for e in which:
            if e in events:
                y_second(e)

    if nz > 3:
        z_round(2)
    x_first(0)
    y_first_if(1)
    far_in(0)
    y_first_if(2)
    far_in(1)
    y_second(0)
    y_first_if(3)
    far_in(2)
    x_far_first(0)
    y_first_if(4)
    far_in(3)
    x_far_first(1)
    y_second_if(1, 2)
    x_far_first(2)
    y_first_if(5, 6)
    x_far_first(3)

    for o in range(1, nch):
        origin = (ch + nch - o) % nch
        arrived(
            note_all.at[origin], (note_sem.at[0, ch], note_sem.at[1, origin]), {"ch": origin}
        )
    note_all[ch] = note_own[...]
    total = note_all[0, 0:1, :]
    for o in range(1, nch):
        total = total + note_all[o, 0:1, :]
    factor = lax.rsqrt(total / float(width * nch) + EPSILON)
    scale[...] = jnp.broadcast_to(factor, (128, tokens)).T

    per_tile = 256
    per_row = nch // ny

    def block_product(block):
        gain = note_all[block, 1:2, :]
        for tile in range(width // 128):
            cols = pl.ds(tile * 128, 128)
            wide = feats[block, :, cols].astype(F32) * scale[...]
            half_norm[:, cols] = (wide * gain[:, tile * 128 : (tile + 1) * 128]).astype(BF16)
        rows = pl.ds(pl.multiple_of(block * width, width), width)

        def columns(j, inner):
            cols = pl.ds(pl.multiple_of(j * per_tile, per_tile), per_tile)
            made = jnp.dot(half_norm[...], weights[rows, cols], preferred_element_type=F32)
            acc[HALO:, cols] += made
            return inner

        lax.fori_loop(0, acc.shape[1] // per_tile, columns, 0)

    def early(block):
        same = block // nx == h
        return same if per_row == 0 else jnp.logical_and(same, block // per_row != (y + 2) % ny)

    def product_if(wanted):
        def body(block, carry):
            @pl.when(wanted(block))
            def _():
                block_product(block)

            return carry

        lax.fori_loop(0, nch, body, 0)

    acc[...] = jnp.zeros_like(acc)
    x_second(0)
    for e in events:
        pair_in(e, (0, 1, 2))
    y_second_if(3, 4)
    if per_row > 0 and ny > 1:
        product_if(early)
    elif ny == 1:
        product_if(lambda block: block // nx == h)
    y_second_if(5, 6)
    if nh > 1:
        for k in range(far_parts):
            x_second(1 + k)
    for e in events:
        pair_in(e, (3, 4))
    if per_row > 0 and ny > 1:
        product_if(lambda block: jnp.logical_not(early(block)))
    elif ny == 1:
        product_if(lambda block: block // nx != h)
    else:
        block_product(0)

    for tile in range(acc.shape[1] // 256):
        cols = pl.ds(tile * 256, 256)
        last = acc[tokens:, cols].astype(BF16)
        tail_out[:, cols] = last
        acc[tokens:, cols] = last.astype(F32)

    @pl.when(ctx < last_ctx)
    def _():
        send(
            lambda: (tail_out, tail_in, sems_of(tail_sem), {"ctx": ctx + 1}),
            lambda: ctx < last_ctx,
        )

    for tile in range(acc.shape[1] // 256):
        cols = pl.ds(tile * 256, 256)
        acc[HALO:tokens, cols] = acc[HALO:tokens, cols].astype(BF16).astype(F32)

    @pl.when(ctx > 0)
    def _():
        arrived(tail_in, (tail_sem.at[0], tail_sem.at[1]), {"ctx": ctx - 1})
        acc[0:HALO, :] = tail_in[...].astype(F32)

    def mixed2(i, base, count, tile):
        cols = pl.ds(i * width + tile * 128, 128)
        at = pl.ds(tile * 128, 128)
        total = None
        for back in range(3):
            term = (
                mtaps_ref[back, i : i + 1, at]
                * acc[base - back : base - back + count, cols]
            )
            total = term if total is None else total + term
        return total

    for tile in range(width // 128):
        cols = pl.ds(tile * 128, 128)
        for base in range(HALO - 128, HALO + tokens, 128):
            made = mixed2(1, base, 128, tile) * mixed2(2, base, 128, tile)
            prod2[base - HALO + 128 : base - HALO + 256, cols] = made.astype(BF16)
            if base >= HALO:
                query[base - HALO : base - HALO + 128, cols] = mixed2(0, base, 128, tile)
    for tile in range(width // 128):
        lines = pl.ds(tile * 128, 128)
        made = lax.dot_general(
            perm[lines, :], prod2[...], (((1,), (1,)), ((), ())), preferred_element_type=F32
        )
        turned[lines, :] = made.astype(BF16)

    members = width // 32

    def one_group(g, carry):
        lines = pl.ds(pl.multiple_of(g * members, members), members)
        data = jnp.concatenate(
            [turned[lines, n * 128 : n * 128 + 256] for n in range(tokens // 128)], axis=0
        )
        made = jnp.dot(data, toep[g], preferred_element_type=F32)
        upper = made.astype(BF16)
        lower = (made - upper.astype(F32)).astype(BF16)
        for n in range(tokens // 128):
            conv_hi[lines, n * 128 : (n + 1) * 128] = upper[n * members : (n + 1) * members]
            conv_lo[lines, n * 128 : (n + 1) * 128] = lower[n * members : (n + 1) * members]
        return carry

    lax.fori_loop(0, 32, one_group, 0)
    flip = (((0,), (0,)), ((), ()))
    for tile in range(width // 256):
        cols = pl.ds(tile * 256, 256)
        made = lax.dot_general(conv_hi[...], perm[:, cols], flip, preferred_element_type=F32)
        made = made + lax.dot_general(
            conv_lo[...], perm[:, cols], flip, preferred_element_type=F32
        )
        made = made + mskip_ref[:, cols] * prod2[128:, cols].astype(F32)
        out_ref[:, cols] = (resid[:, cols] + query[:, cols] * made).astype(BF16)

    for make, cond in waits:
        if cond is None:
            copy(*make()).wait_send()
        else:
            pl.when(cond())(lambda make=make: copy(*make()).wait_send())


def local(sizes, *arrays):
    (
        token_ids,
        embedding,
        long_table,
        long_taps,
        long_residue,
        long_rate,
        long_skip,
        medium_gain,
        medium_weight,
        medium_taps,
        medium_group_filter,
        medium_skip,
        filter_group,
    ) = arrays
    ny, nz, nh, nx = sizes
    nch, nctx = nh * nx, 2 * ny * nz
    tokens, width = token_ids.shape[0], embedding.shape[1]
    piece = medium_weight.shape[0]
    events = 1 + 2 * (nz - 1)
    hops = max(nz - 1, 1)
    vmem = pl.BlockSpec(memory_space=pltpu.VMEM)
    hbm = pl.BlockSpec(memory_space=pl.ANY)
    dma = pltpu.SemaphoreType.DMA
    return pl.pallas_call(
        functools.partial(kernel, sizes),
        out_shape=jax.ShapeDtypeStruct((tokens, width), BF16),
        in_specs=[vmem, hbm, hbm] + [vmem] * 5 + [hbm] + [vmem] * 4,
        out_specs=vmem,
        scratch_shapes=[
            pltpu.VMEM((32, width), BF16),
            pltpu.VMEM((3, 32, width), BF16),
            pltpu.VMEM((8, tokens), jnp.int32),
            pltpu.VMEM((nctx * piece, 3 * width), BF16),
            pltpu.VMEM((nch, tokens, width), BF16),
            pltpu.VMEM((HALO + tokens, 3 * width), F32),
            pltpu.VMEM((3, tokens, 32), BF16),
            pltpu.VMEM((8, 128), jnp.int32),
            pltpu.VMEM((width // 128, tokens, 128), F32),
            pltpu.VMEM((tokens, width), F32),
            pltpu.VMEM((tokens, width), F32),
            pltpu.VMEM((width // 128, tokens, 128), F32),
            pltpu.VMEM((32, width), F32),
            pltpu.VMEM((16, 8, width), F32),
            pltpu.VMEM((16, width), F32),
            pltpu.VMEM((16, width), F32),
            pltpu.VMEM((16, width), F32),
            pltpu.VMEM((nz, 16, width), F32),
            pltpu.VMEM((16, width), F32),
            pltpu.VMEM((ny, 16, width), F32),
            pltpu.VMEM((8, tokens), F32),
            pltpu.VMEM((nch, 8, tokens), F32),
            pltpu.VMEM((tokens, 128), F32),
            pltpu.VMEM((tokens, width), BF16),
            pltpu.VMEM((width, width), BF16),
            pltpu.VMEM((32, 256, 128), BF16),
            pltpu.VMEM((HALO, 3 * width), BF16),
            pltpu.VMEM((HALO, 3 * width), BF16),
            pltpu.VMEM((128 + tokens, width), BF16),
            pltpu.VMEM((width, 128 + tokens), BF16),
            pltpu.VMEM((width, tokens), BF16),
            pltpu.VMEM((width, tokens), BF16),
            dma((5,)),
            dma((2,)),
            dma((2, hops, 2)),
            dma((2, events, 4)),
            dma((2, events, 5)),
            dma((2,)),
            dma((2, nz)),
            dma((2, ny)),
            dma((2, nch)),
            dma((2, 5, 4)),
            dma((2, 4)),
            dma((2,)),
        ],
        compiler_params=pltpu.CompilerParams(
            collective_id=0, has_side_effects=True, vmem_limit_bytes=60 << 20
        ),
    )(
        token_ids[None],
        embedding,
        jnp.transpose(long_table, (1, 0, 2)),
        long_taps,
        long_residue.T,
        long_rate.T,
        long_skip[None],
        medium_gain[None],
        jnp.transpose(medium_weight, (1, 0, 2)),
        medium_taps,
        medium_group_filter,
        medium_skip[None],
        filter_group[None],
    )


def solution(mesh, sizes=(4, 4, 2, 4)):
    in_specs = (
        P("ctx"),
        P(None, "ch"),
        P(None, None, "ch"),
        P(None, None, "ch"),
        P("ch", None),
        P("ch", None),
        P("ch"),
        P("ch"),
        P("ctx", None, "ch"),
        P(None, None, "ch"),
        P("ch", None),
        P("ch"),
        P("ch"),
    )
    return jax.shard_map(
        functools.partial(local, sizes),
        mesh=mesh,
        in_specs=in_specs,
        out_specs=P("ctx", "ch"),
        check_vma=False,
    )
```

```python
import functools

import jax
import jax.numpy as jnp
from jax import lax
from jax.experimental import pallas as pl
from jax.experimental.pallas import tpu as pltpu
from jax.sharding import PartitionSpec as P

EPSILON = 1e-06
HALO = 144
F32 = jnp.float32
BF16 = jnp.bfloat16


def kernel(
    sizes,
    token_ref,
    emb_ref,
    table_ref,
    ltaps_ref,
    residue_ref,
    rate_ref,
    lskip_ref,
    gain_ref,
    w_ref,
    mtaps_ref,
    filt_ref,
    mskip_ref,
    group_ref,
    out_ref,
    emb,
    table,
    tok_ref,
    weights,
    feats,
    acc,
    hot,
    halo_tok,
    prod,
    query,
    resid,
    conv,
    chan,
    excl,
    end_own,
    end_other,
    chip_own,
    chip_all,
    row_own,
    row_all,
    note_own,
    note_all,
    scale,
    half_norm,
    perm,
    toep,
    tail_out,
    tail_in,
    prod2,
    turned,
    conv_hi,
    conv_lo,
    load_sem,
    tok_sem,
    z_sem,
    y_sem,
    pair_sem,
    end_sem,
    chip_sem,
    row_sem,
    note_sem,
    x_sem,
    far_sem,
    tail_sem,
):
    ny, nz, nh, nx = sizes
    nch = nh * nx
    tokens, width = query.shape
    piece = w_ref.shape[1]
    ctx, ch = lax.axis_index("ctx"), lax.axis_index("ch")
    core, chip = ctx % 2, ctx // 2
    z, y = chip % nz, chip // nz
    x, h = ch % nx, ch // nx
    last_ctx = 2 * ny * nz - 1
    waits = []

    def along(yy, zz, cc):
        return {"ctx": (yy * nz + zz) * 2 + cc}

    def across(hh, xx):
        return {"ch": hh * nx + xx}

    def copy(src, dst, sems, to):
        made = pltpu.make_async_remote_copy(
            src_ref=src,
            dst_ref=dst,
            send_sem=sems[0],
            recv_sem=sems[1],
            device_id=to,
            device_id_type=pl.DeviceIdType.MESH,
        )
        return made

    def send(make, cond=None):
        copy(*make()).start()
        waits.append((make, cond))

    def sems_of(ref, *index):
        return ref.at[(0, *index)], ref.at[(1, *index)]

    def arrived(dst, sems, to):
        copy(dst, dst, sems, to).wait_recv()

    barrier = pltpu.get_barrier_semaphore()
    peers = [along(y, z, 1 - core)]
    peers += [along(y, (z + o) % nz, core) for o in range(1, nz)]
    peers += [along((y + o) % ny, z, core) for o in range(1, ny)]
    peers += [{"ch": (ch + o) % nch} for o in range(1, nch)]
    for peer in peers:
        pl.semaphore_signal(barrier, inc=1, device_id=peer, device_id_type=pl.DeviceIdType.MESH)
    has_next = jnp.logical_and(core == 1, ctx < last_ctx)
    has_before = jnp.logical_and(core == 0, ctx > 0)

    @pl.when(has_next)
    def _():
        pl.semaphore_signal(
            barrier, inc=1, device_id={"ctx": ctx + 1}, device_id_type=pl.DeviceIdType.MESH
        )

    @pl.when(has_before)
    def _():
        pl.semaphore_signal(
            barrier, inc=1, device_id={"ctx": ctx - 1}, device_id_type=pl.DeviceIdType.MESH
        )

    def rows_of(slot):
        return pl.ds(pl.multiple_of(slot * piece, piece), piece)

    def part_of(slot, part):
        return pl.ds(pl.multiple_of(slot * piece + part * (piece // 2), piece // 2), piece // 2)

    loads = [
        pltpu.make_async_copy(
            w_ref.at[i], weights.at[rows_of(ctx), pl.ds(i * width, width)], load_sem.at[i]
        )
        for i in range(3)
    ]
    loads.append(pltpu.make_async_copy(emb_ref.at[pl.ds(64, 32)], emb, load_sem.at[3]))
    loads.append(pltpu.make_async_copy(table_ref.at[:, pl.ds(64, 32)], table, load_sem.at[4]))
    for load in loads:
        load.start()
    tok_ref[...] = jnp.broadcast_to(token_ref[...], tok_ref.shape)

    def slot(yy, zz, cc):
        return (yy * nz + zz) * 2 + cc

    def event_of(e):
        if e == 0:
            return z, None
        r = (e - 1) // 2
        if e % 2 == 1:
            return z - 1 - r, lambda: z - 1 - r >= 0
        return z + 1 + r, lambda: z + 1 + r < nz

    def guarded(cond, body):
        if cond is None:
            body()
        else:
            pl.when(cond())(body)

    up, down = (y + 1) % ny, (y + ny - 1) % ny

    def pair(e, kind, rows, cond):
        def make():
            view = weights.at[rows()]
            return view, view, sems_of(pair_sem, e, kind), along(y, z, 1 - core)

        send(make, cond)

    def y_sends(e, zz, cond):
        if ny > 1:
            for way, to in ((0, up), (1, down)):

                def make(way=way, to=to):
                    view = weights.at[rows_of(slot(y, zz, core))]
                    return view, view, sems_of(y_sem, e, way), along(to, z, core)

                send(make, cond)

    def z_send(way, hop, zz, cond):
        def inside():
            return z + 1 < nz if way == 0 else z > 0

        def wanted():
            return inside() if cond is None else jnp.logical_and(cond(), inside())

        def make():
            view = weights.at[rows_of(slot(y, zz, core))]
            to = z + 1 if way == 0 else z - 1
            return view, view, sems_of(z_sem, hop, way), along(y, to, core)

        pl.when(inside())(lambda: send(make, wanted))

    def own_weights():
        if nz > 1:
            z_send(0, 0, z, None)
            z_send(1, 0, z, None)
        y_sends(0, z, None)
        pair(0, 0, lambda: rows_of(slot(y, z, core)), None)

    def z_forward(r):
        for way in (0, 1):
            e = 1 + 2 * r + way
            zz, valid = event_of(e)

            def body(way=way, e=e, zz=zz, valid=valid):
                rows = rows_of(slot(y, zz, core))
                arrived(
                    weights.at[rows],
                    (z_sem.at[0, r, way], z_sem.at[1, r, way]),
                    along(y, zz, core),
                )
                if r + 1 < nz - 1:
                    z_send(way, r + 1, zz, valid)

            guarded(valid, body)

    def z_spread(r):
        for way in (0, 1):
            e = 1 + 2 * r + way
            zz, valid = event_of(e)

            def body(e=e, zz=zz, valid=valid):
                y_sends(e, zz, valid)
                pair(e, 0, lambda: rows_of(slot(y, zz, core)), valid)

            guarded(valid, body)

    def z_round(r):
        z_forward(r)
        z_spread(r)

    def y_first(e):
        zz, valid = event_of(e)

        def body():
            for way, origin, to in ((0, down, up), (1, up, down)):
                rows = rows_of(slot(origin, zz, core))
                arrived(
                    weights.at[rows],
                    (y_sem.at[0, e, way], y_sem.at[1, e, way]),
                    along(origin, z, core),
                )

                def make(way=way, origin=origin, to=to):
                    view = weights.at[part_of(slot(origin, zz, core), way)]
                    return view, view, sems_of(y_sem, e, 2 + way), along(to, z, core)

                send(make, valid)
                pair(e, 1 + way, lambda origin=origin: rows_of(slot(origin, zz, core)), valid)

        if ny > 1:
            guarded(valid, body)

    def y_second(e):
        zz, valid = event_of(e)

        def body():
            for way, origin in ((0, down), (1, up)):
                half = part_of(slot((y + 2) % ny, zz, core), way)
                arrived(
                    weights.at[half],
                    (y_sem.at[0, e, 2 + way], y_sem.at[1, e, 2 + way]),
                    along(origin, z, core),
                )
                pair(
                    e, 3 + way, lambda way=way: part_of(slot((y + 2) % ny, zz, core), way), valid
                )

        if ny > 1:
            guarded(valid, body)

    def pair_in(e, kinds):
        zz, valid = event_of(e)

        def body():
            other = along(y, z, 1 - core)

            def one(kind, rows):
                if kind in kinds:
                    arrived(weights.at[rows], sems_of(pair_sem, e, kind), other)

            one(0, rows_of(slot(y, zz, 1 - core)))
            if ny > 1:
                one(1, rows_of(slot(down, zz, 1 - core)))
                one(2, rows_of(slot(up, zz, 1 - core)))
                one(3, part_of(slot((y + 2) % ny, zz, 1 - core), 0))
                one(4, part_of(slot((y + 2) % ny, zz, 1 - core), 1))

        guarded(valid, body)

    events = list(range(1 + 2 * (nz - 1)))

    group_row = (group_ref[...] - ch * (width // 16)).astype(F32)
    of_group = (
        lax.broadcasted_iota(jnp.int32, (32, width), 0).astype(F32) == group_row
    ).astype(F32)
    rate_in = rate_ref[...]
    twice = 2.0 * rate_in
    series = jnp.ones_like(twice)
    for k in range(9, 1, -1):
        series = 1.0 - twice * (1.0 / k) * series
    both = jnp.concatenate([rate_in, residue_ref[...] * jnp.sqrt(twice * series)], axis=0)
    chan[...] = jnp.dot(
        both, of_group, precision=lax.Precision.HIGHEST, preferred_element_type=F32
    )

    def one_hots(joined, count):
        codes = 64 + lax.broadcasted_iota(jnp.int32, (32, count), 0)
        for back in range(3):
            shifted = joined if back == 0 else pltpu.roll(joined, back, 1)
            row = shifted[0:1, 128:]
            hot[back, 0:count] = (row == codes).astype(F32).T.astype(BF16)

    def streams(rows):
        for tile in range(width // 128):
            cols = pl.ds(tile * 128, 128)

            def mixed(i, cols=cols):
                total = None
                for back in range(3):
                    picked = jnp.dot(
                        hot[back, 0:rows], table[i, :, cols], preferred_element_type=F32
                    )
                    term = ltaps_ref[back, i : i + 1, cols] * picked
                    total = term if total is None else total + term
                return total

            key = mixed(1)
            prod[tile, 0:rows] = (key * mixed(2)).astype(BF16).astype(F32)
            query[0:rows, cols] = mixed(0)

    one_hots(jnp.concatenate([jnp.full((8, 128), -1, jnp.int32), tok_ref[...]], axis=1), tokens)
    loads[3].wait()
    loads[4].wait()
    resid[...] = jnp.dot(hot[0], emb[...], preferred_element_type=F32)
    streams(tokens)

    extra = jnp.logical_or(has_next, has_before)
    pl.semaphore_wait(barrier, len(peers) + extra.astype(jnp.int32))
    tail_tok = pl.ds(tokens - 128, 128)

    @pl.when(ctx < last_ctx)
    def _():
        send(
            lambda: (tok_ref.at[:, tail_tok], halo_tok, sems_of(tok_sem), {"ctx": ctx + 1}),
            lambda: ctx < last_ctx,
        )

    for load in loads[:3]:
        load.wait()
    own_weights()

    taps = filt_ref.shape[1]

    def make_toep(g, carry):
        line = filt_ref[pl.ds(g, 1), :]
        line = jnp.concatenate([line, jnp.zeros((1, taps), F32)], axis=1)
        spread = jnp.broadcast_to(line, (2 * taps, 2 * taps))
        turned_line = pltpu.roll(spread, taps, 1, stride=1, stride_axis=0)
        toep[g] = turned_line[:, :taps].astype(BF16)
        return carry

    lax.fori_loop(0, filt_ref.shape[0], make_toep, 0)
    lanes = lax.broadcasted_iota(jnp.int32, (128, width), 1)
    rank = jnp.zeros((1, width), F32)
    group_col = jnp.broadcast_to(group_row, (128, width)).T
    for tile in range(width // 128):
        mine = group_col[tile * 128 : (tile + 1) * 128, 0:1]
        above = tile * 128 + lax.broadcasted_iota(jnp.int32, (128, width), 0) < lanes
        same = jnp.logical_and(mine == group_row, above)
        rank = rank + jnp.sum(same.astype(F32), axis=0, keepdims=True)
    placed = group_row * float(width // 32) + rank
    for tile in range(width // 128):
        place = (tile * 128 + lax.broadcasted_iota(jnp.int32, (128, width), 0)).astype(F32)
        perm[tile * 128 : (tile + 1) * 128, :] = (place == placed).astype(F32).astype(BF16)

    @pl.when(ctx > 0)
    def _():
        arrived(halo_tok, (tok_sem.at[0], tok_sem.at[1]), {"ctx": ctx - 1})
        one_hots(jnp.concatenate([halo_tok[...], tok_ref[:, 0:128]], axis=1), 128)
        streams(16)

    chunk = tokens // 8
    chunk_id = lax.broadcasted_iota(jnp.int32, (8, 128), 0)

    def row_b(ref, p, cols):
        return jnp.broadcast_to(ref[p : p + 1, cols], (8, 128))

    for tile in range(width // 128):
        cols = pl.ds(tile * 128, 128)
        decay = [jnp.exp(-row_b(chan, p, cols)) for p in range(16)]

        def step(k, states, tile=tile, decay=decay):
            row = prod[tile, pl.ds(k, 8, stride=chunk), :]
            return tuple(d * s + row for d, s in zip(decay, states))

        states = lax.fori_loop(
            0, chunk, step, tuple(jnp.zeros((8, 128), F32) for _ in range(16)), unroll=4
        )
        for p in range(16):
            rate = row_b(chan, p, cols) * float(chunk)
            total = states[p]
            for by in (1, 2, 4):
                moved = jnp.exp(-rate * float(by)) * pltpu.roll(total, by, 0)
                total = total + jnp.where(chunk_id >= by, moved, 0.0)
            end_own[p : p + 1, cols] = total[7:8]
            excl[p, :, cols] = jnp.where(chunk_id >= 1, pltpu.roll(total, 1, 0), 0.0)

    rates = chan[0:16, :]
    send(lambda: (end_own, end_other, sems_of(end_sem), along(y, z, 1 - core)))
    arrived(end_other, (end_sem.at[0], end_sem.at[1]), along(y, z, 1 - core))
    first = jnp.where(core == 0, end_own[...], end_other[...])
    second = jnp.where(core == 0, end_other[...], end_own[...])
    decay_dev = jnp.exp(-rates * float(tokens))
    chip_own[...] = first * decay_dev + second
    for o in range(1, nz):
        send(
            lambda o=o: (
                chip_own,
                chip_all.at[z],
                (chip_sem.at[0, (z + o) % nz], chip_sem.at[1, z]),
                along(y, (z + o) % nz, core),
            )
        )
    if nz > 1:
        z_forward(0)
    y_first(0)
    for o in range(1, nz):
        origin = (z + nz - o) % nz
        arrived(
            chip_all.at[origin], (chip_sem.at[0, z], chip_sem.at[1, origin]), along(y, origin, core)
        )
    decay_chip = jnp.exp(-rates * float(2 * tokens))
    whole = None
    for zz in range(nz):
        if nz == 1:
            this = chip_own[...]
        else:
            this = jnp.where(z == zz, chip_own[...], chip_all[zz])
        whole = this if whole is None else whole * decay_chip + this
    row_own[...] = whole
    for o in range(1, ny):

        @pl.when(y + o < ny)
        def _(o=o):
            send(
                lambda: (
                    row_own,
                    row_all.at[y],
                    (row_sem.at[0, (y + o) % ny], row_sem.at[1, y]),
                    along((y + o) % ny, z, core),
                ),
                lambda: y + o < ny,
            )

    if nz > 1:
        z_spread(0)
    for o in range(1, ny):

        @pl.when(y >= o)
        def _(o=o):
            origin = (y + ny - o) % ny
            arrived(
                row_all.at[origin],
                (row_sem.at[0, y], row_sem.at[1, origin]),
                along(origin, z, core),
            )

    decay_row = jnp.exp(-rates * float(2 * tokens * nz))
    carried = jnp.zeros((16, width), F32)
    for yy in range(ny - 1):
        carried = jnp.where(yy < y, carried * decay_row + row_all[yy], carried)
    for zz in range(nz - 1):
        carried = jnp.where(zz < z, carried * decay_chip + chip_all[zz], carried)
    carried = jnp.where(core == 1, carried * decay_dev + first, carried)
    end_other[...] = carried

    for tile in range(width // 128):
        cols = pl.ds(tile * 128, 128)
        start = []
        for p in range(16):
            rate = row_b(chan, p, cols) * float(chunk)
            start.append(
                excl[p, :, cols]
                + jnp.exp(-rate * chunk_id.astype(F32)) * row_b(end_other, p, cols)
            )
        decay = [jnp.exp(-row_b(chan, p, cols)) for p in range(16)]
        weigh = [row_b(chan, 16 + p, cols) for p in range(16)]

        def step2(k, states, tile=tile, decay=decay, weigh=weigh):
            where = pl.ds(k, 8, stride=chunk)
            row = prod[tile, where, :]
            states = tuple(d * s + row for d, s in zip(decay, states))
            sums = [None] * 4
            for p in range(16):
                term = weigh[p] * states[p]
                sums[p % 4] = term if sums[p % 4] is None else sums[p % 4] + term
            conv[tile, where, :] = (sums[0] + sums[1]) + (sums[2] + sums[3])
            return states

        lax.fori_loop(0, chunk, step2, tuple(start), unroll=2)

    squares = None
    for tile in range(width // 128):
        cols = pl.ds(tile * 128, 128)
        whole = conv[tile] + lskip_ref[:, cols] * prod[tile]
        middle = (resid[:, cols] + query[:, cols] * whole).astype(BF16)
        feats[ch, :, cols] = middle
        wide = middle.astype(F32)
        resid[:, cols] = wide
        squares = wide * wide if squares is None else squares + wide * wide
    note_own[...] = jnp.broadcast_to(jnp.sum(squares.T, axis=0, keepdims=True), note_own.shape)
    note_own[1:2, :] = gain_ref[...].astype(F32)
    for o in range(1, nch):
        send(
            lambda o=o: (
                note_own,
                note_all.at[ch],
                (note_sem.at[0, (ch + o) % nch], note_sem.at[1, ch]),
                {"ch": (ch + o) % nch},
            )
        )

    right, left = (x + 1) % nx, (x + nx - 1) % nx
    far_parts = 4
    far_rows = tokens // far_parts

    def rows_x(e):
        return (0, tokens) if e == 0 else ((e - 1) * far_rows, far_rows)

    def half_x(e, way):
        base, count = rows_x(e)
        return pl.ds(base + way * (count // 2), count // 2)

    def x_sends(e):
        if nx > 1:
            for way, to in ((0, right), (1, left)):

                def make(way=way, to=to):
                    view = feats.at[side(e) * nx + x, pl.ds(*rows_x(e))]
                    return view, view, sems_of(x_sem, e, way), across(h, to)

                send(make)

    def side(e):
        return h if e == 0 else 1 - h

    def x_first(e):
        if nx > 1:
            for way, origin, to in ((0, left, right), (1, right, left)):
                block = side(e) * nx + origin
                arrived(
                    feats.at[block, pl.ds(*rows_x(e))], sems_of(x_sem, e, way), across(h, origin)
                )

                def make(way=way, block=block, to=to):
                    part = feats.at[block, half_x(e, way)]
                    return part, part, sems_of(x_sem, e, 2 + way), across(h, to)

                send(make)

    def x_second(e):
        if nx > 1:
            for way, origin in ((0, left), (1, right)):
                part = feats.at[side(e) * nx + (x + 2) % nx, half_x(e, way)]
                arrived(part, sems_of(x_sem, e, 2 + way), across(h, origin))

    def far_in(k):
        if nh > 1:
            part = feats.at[(1 - h) * nx + x, pl.ds(k * far_rows, far_rows)]
            arrived(part, sems_of(far_sem, k), across(1 - h, x))
            x_sends(1 + k)

    def x_far_first(k):
        if nh > 1:
            x_first(1 + k)

    x_sends(0)
    for r in range(1, nz - 1):
        z_round(r)
    if nh > 1:
        for k in range(far_parts):

            def make(k=k):
                part = feats.at[ch, pl.ds(k * far_rows, far_rows)]
                return part, part, sems_of(far_sem, k), across(1 - h, x)

            send(make)

    def y_first_if(*which):
        for e in which:
            if e in events:
                y_first(e)

    def y_second_if(*which):
        for e in which:
            if e in events:
                y_second(e)

    acc[...] = jnp.zeros_like(acc)
    x_first(0)
    y_first_if(1, 2)
    y_second(0)
    far_in(0)
    far_in(1)
    x_far_first(0)
    y_first_if(3, 4)
    far_in(2)
    x_far_first(1)
    far_in(3)
    y_first_if(5, 6)

    for o in range(1, nch):
        origin = (ch + nch - o) % nch
        arrived(
            note_all.at[origin], (note_sem.at[0, ch], note_sem.at[1, origin]), {"ch": origin}
        )
    note_all[ch] = note_own[...]
    total = note_all[0, 0:1, :]
    for o in range(1, nch):
        total = total + note_all[o, 0:1, :]
    factor = lax.rsqrt(total / float(width * nch) + EPSILON)
    scale[...] = jnp.broadcast_to(factor, (128, tokens)).T

    per_tile = 256
    per_row = nch // ny
    wide_all = acc.shape[1]

    def block_product(block, top, count):
        gain = note_all[block, 1:2, :]
        for tile in range(width // 128):
            cols = pl.ds(tile * 128, 128)
            wide = feats[block, top : top + count, cols].astype(F32) * scale[top : top + count, :]
            half_norm[top : top + count, cols] = (
                wide * gain[:, tile * 128 : (tile + 1) * 128]
            ).astype(BF16)
        rows = pl.ds(pl.multiple_of(block * width, width), width)
        for tile in range(wide_all // per_tile):
            cols = pl.ds(tile * per_tile, per_tile)
            acc[HALO + top : HALO + top + count, cols] += jnp.dot(
                half_norm[top : top + count, :], weights[rows, cols], preferred_element_type=F32
            )

    def early(block):
        same = block // nx == h
        if ny == 1:
            return same
        return jnp.logical_and(same, block // per_row != (y + 2) % ny)

    def late(block):
        return jnp.logical_not(early(block))

    def product_if(wanted, first, count, top, rows):
        def body(i, carry):
            block = first + i

            @pl.when(wanted(block))
            def _():
                block_product(block, top, rows)

            return carry

        lax.fori_loop(0, count, body, 0)

    split = nch > 1
    x_second(0)
    for e in events:
        pair_in(e, (0, 1, 2))
    x_far_first(2)
    if split:
        product_if(early, h * nx, nx // 2, 0, tokens)
    x_far_first(3)
    y_second_if(1, 2)
    if split:
        product_if(early, h * nx + nx // 2, nx // 2, 0, tokens)
    y_second_if(3, 4, 5, 6)
    if nh > 1:
        for k in range(far_parts):
            x_second(1 + k)
    for e in events:
        pair_in(e, (3, 4))

    body_rows = tokens - HALO
    if split:
        product_if(late, 0, nch, body_rows, HALO)
    else:
        block_product(0, body_rows, HALO)
    for tile in range(wide_all // 256):
        cols = pl.ds(tile * 256, 256)
        last = acc[tokens:, cols].astype(BF16)
        tail_out[:, cols] = last
        acc[tokens:, cols] = last.astype(F32)
    tail_parts = (
        (pl.ds(0, HALO), pl.ds(width, 2 * width)),
        (pl.ds(HALO - 16, 16), pl.ds(0, width)),
    )

    @pl.when(ctx < last_ctx)
    def _():
        for k, part in enumerate(tail_parts):
            send(
                lambda k=k, part=part: (
                    tail_out.at[part],
                    tail_in.at[part],
                    sems_of(tail_sem, k),
                    {"ctx": ctx + 1},
                ),
                lambda: ctx < last_ctx,
            )

    if split:
        product_if(late, 0, nch, 0, body_rows)
    else:
        block_product(0, 0, body_rows)
    for tile in range(wide_all // 256):
        cols = pl.ds(tile * 256, 256)
        acc[HALO:tokens, cols] = acc[HALO:tokens, cols].astype(BF16).astype(F32)

    def mixed2(i, base, count, tile):
        cols = pl.ds(i * width + tile * 128, 128)
        at = pl.ds(tile * 128, 128)
        total = None
        for back in range(3):
            term = (
                mtaps_ref[back, i : i + 1, at]
                * acc[base - back : base - back + count, cols]
            )
            total = term if total is None else total + term
        return total

    members = width // 32
    flip = (((0,), (0,)), ((), ()))

    def products(bases):
        for tile in range(width // 128):
            cols = pl.ds(tile * 128, 128)
            for base in bases:
                made = mixed2(1, base, 128, tile) * mixed2(2, base, 128, tile)
                prod2[base - HALO + 128 : base - HALO + 256, cols] = made.astype(BF16)
                if base >= HALO:
                    query[base - HALO : base - HALO + 128, cols] = mixed2(0, base, 128, tile)
        top, end = bases[0] - HALO + 128, bases[-1] - HALO + 256
        for tile in range(width // 128):
            lines = pl.ds(tile * 128, 128)
            made = lax.dot_general(
                perm[lines, :],
                prod2[top:end, :],
                (((1,), (1,)), ((), ())),
                preferred_element_type=F32,
            )
            turned[lines, top:end] = made.astype(BF16)

    def filtered(blocks):
        def one_group(g, carry):
            lines = pl.ds(pl.multiple_of(g * members, members), members)
            data = jnp.concatenate(
                [turned[lines, n * 128 : n * 128 + 256] for n in blocks], axis=0
            )
            made = jnp.dot(data, toep[g], preferred_element_type=F32)
            upper = made.astype(BF16)
            lower = (made - upper.astype(F32)).astype(BF16)
            for k, n in enumerate(blocks):
                conv_hi[lines, n * 128 : (n + 1) * 128] = upper[k * members : (k + 1) * members]
                conv_lo[lines, n * 128 : (n + 1) * 128] = lower[k * members : (k + 1) * members]
            return carry

        lax.fori_loop(0, 32, one_group, 0, unroll=4)
        top, end = blocks[0] * 128, (blocks[-1] + 1) * 128
        for tile in range(width // 256):
            cols = pl.ds(tile * 256, 256)
            made = lax.dot_general(
                conv_hi[:, top:end], perm[:, cols], flip, preferred_element_type=F32
            )
            made = made + lax.dot_general(
                conv_lo[:, top:end], perm[:, cols], flip, preferred_element_type=F32
            )
            made = made + mskip_ref[:, cols] * prod2[128 + top : 128 + end, cols].astype(F32)
            out_ref[top:end, cols] = (
                resid[top:end, cols] + query[top:end, cols] * made
            ).astype(BF16)

    products([HALO + 128, HALO + 256, HALO + 384])
    filtered((2, 3))
    for make, cond in waits:
        if cond is None:
            copy(*make()).wait_send()
        else:
            pl.when(cond())(lambda make=make: copy(*make()).wait_send())

    @pl.when(ctx > 0)
    def _():
        for k, part in enumerate(tail_parts):
            arrived(tail_in.at[part], sems_of(tail_sem, k), {"ctx": ctx - 1})
        acc[0:HALO, width:] = tail_in[:, width:].astype(F32)
        acc[HALO - 16 : HALO, 0:width] = tail_in[HALO - 16 :, 0:width].astype(F32)

    products([HALO - 128, HALO])
    filtered((0, 1))


def local(sizes, *arrays):
    (
        token_ids,
        embedding,
        long_table,
        long_taps,
        long_residue,
        long_rate,
        long_skip,
        medium_gain,
        medium_weight,
        medium_taps,
        medium_group_filter,
        medium_skip,
        filter_group,
    ) = arrays
    ny, nz, nh, nx = sizes
    nch, nctx = nh * nx, 2 * ny * nz
    tokens, width = token_ids.shape[0], embedding.shape[1]
    piece = medium_weight.shape[0]
    events = 1 + 2 * (nz - 1)
    hops = max(nz - 1, 1)
    vmem = pl.BlockSpec(memory_space=pltpu.VMEM)
    hbm = pl.BlockSpec(memory_space=pl.ANY)
    dma = pltpu.SemaphoreType.DMA
    return pl.pallas_call(
        functools.partial(kernel, sizes),
        out_shape=jax.ShapeDtypeStruct((tokens, width), BF16),
        in_specs=[vmem, hbm, hbm] + [vmem] * 5 + [hbm] + [vmem] * 4,
        out_specs=vmem,
        scratch_shapes=[
            pltpu.VMEM((32, width), BF16),
            pltpu.VMEM((3, 32, width), BF16),
            pltpu.VMEM((8, tokens), jnp.int32),
            pltpu.VMEM((nctx * piece, 3 * width), BF16),
            pltpu.VMEM((nch, tokens, width), BF16),
            pltpu.VMEM((HALO + tokens, 3 * width), F32),
            pltpu.VMEM((3, tokens, 32), BF16),
            pltpu.VMEM((8, 128), jnp.int32),
            pltpu.VMEM((width // 128, tokens, 128), F32),
            pltpu.VMEM((tokens, width), F32),
            pltpu.VMEM((tokens, width), F32),
            pltpu.VMEM((width // 128, tokens, 128), F32),
            pltpu.VMEM((32, width), F32),
            pltpu.VMEM((16, 8, width), F32),
            pltpu.VMEM((16, width), F32),
            pltpu.VMEM((16, width), F32),
            pltpu.VMEM((16, width), F32),
            pltpu.VMEM((nz, 16, width), F32),
            pltpu.VMEM((16, width), F32),
            pltpu.VMEM((ny, 16, width), F32),
            pltpu.VMEM((8, tokens), F32),
            pltpu.VMEM((nch, 8, tokens), F32),
            pltpu.VMEM((tokens, 128), F32),
            pltpu.VMEM((tokens, width), BF16),
            pltpu.VMEM((width, width), BF16),
            pltpu.VMEM((32, 256, 128), BF16),
            pltpu.VMEM((HALO, 3 * width), BF16),
            pltpu.VMEM((HALO, 3 * width), BF16),
            pltpu.VMEM((128 + tokens, width), BF16),
            pltpu.VMEM((width, 128 + tokens), BF16),
            pltpu.VMEM((width, tokens), BF16),
            pltpu.VMEM((width, tokens), BF16),
            dma((5,)),
            dma((2,)),
            dma((2, hops, 2)),
            dma((2, events, 4)),
            dma((2, events, 5)),
            dma((2,)),
            dma((2, nz)),
            dma((2, ny)),
            dma((2, nch)),
            dma((2, 5, 4)),
            dma((2, 4)),
            dma((2, 2)),
        ],
        compiler_params=pltpu.CompilerParams(
            collective_id=0, has_side_effects=True, vmem_limit_bytes=60 << 20
        ),
    )(
        token_ids[None],
        embedding,
        jnp.transpose(long_table, (1, 0, 2)),
        long_taps,
        long_residue.T,
        long_rate.T,
        long_skip[None],
        medium_gain[None],
        jnp.transpose(medium_weight, (1, 0, 2)),
        medium_taps,
        medium_group_filter,
        medium_skip[None],
        filter_group[None],
    )


def solution(mesh, sizes=(4, 4, 2, 4)):
    in_specs = (
        P("ctx"),
        P(None, "ch"),
        P(None, None, "ch"),
        P(None, None, "ch"),
        P("ch", None),
        P("ch", None),
        P("ch"),
        P("ch"),
        P("ctx", None, "ch"),
        P(None, None, "ch"),
        P("ch", None),
        P("ch"),
        P("ch"),
    )
    return jax.shard_map(
        functools.partial(local, sizes),
        mesh=mesh,
        in_specs=in_specs,
        out_specs=P("ctx", "ch"),
        check_vma=False,
    )
```

```python
import functools

import jax
import jax.numpy as jnp
from jax import lax
from jax.experimental import pallas as pl
from jax.experimental.pallas import tpu as pltpu
from jax.sharding import PartitionSpec as P

EPSILON = 1e-06
HALO = 144
F32 = jnp.float32
BF16 = jnp.bfloat16


def kernel(
    sizes,
    token_ref,
    emb_ref,
    table_ref,
    ltaps_ref,
    residue_ref,
    rate_ref,
    lskip_ref,
    gain_ref,
    w_ref,
    mtaps_ref,
    filt_ref,
    mskip_ref,
    group_ref,
    out_hbm,
    out_ref,
    emb,
    table,
    tok_ref,
    weights,
    feats,
    acc,
    hot,
    halo_tok,
    prod,
    query,
    resid,
    conv,
    chan,
    excl,
    end_own,
    end_other,
    chip_own,
    chip_all,
    row_own,
    row_all,
    note_own,
    note_all,
    scale,
    half_norm,
    perm,
    toep,
    tail_out,
    tail_in,
    prod2,
    turned,
    conv_hi,
    conv_lo,
    load_sem,
    tok_sem,
    z_sem,
    y_sem,
    pair_sem,
    end_sem,
    chip_sem,
    row_sem,
    note_sem,
    x_sem,
    far_sem,
    tail_sem,
    out_sem,
):
    ny, nz, nh, nx = sizes
    nch = nh * nx
    tokens, width = query.shape
    piece = w_ref.shape[1]
    ctx, ch = lax.axis_index("ctx"), lax.axis_index("ch")
    core, chip = ctx % 2, ctx // 2
    z, y = chip % nz, chip // nz
    x, h = ch % nx, ch // nx
    last_ctx = 2 * ny * nz - 1
    waits = []

    def along(yy, zz, cc):
        return {"ctx": (yy * nz + zz) * 2 + cc}

    def across(hh, xx):
        return {"ch": hh * nx + xx}

    def copy(src, dst, sems, to):
        made = pltpu.make_async_remote_copy(
            src_ref=src,
            dst_ref=dst,
            send_sem=sems[0],
            recv_sem=sems[1],
            device_id=to,
            device_id_type=pl.DeviceIdType.MESH,
        )
        return made

    def send(make, cond=None):
        copy(*make()).start()
        waits.append((make, cond))

    def sems_of(ref, *index):
        return ref.at[(0, *index)], ref.at[(1, *index)]

    def arrived(dst, sems, to):
        copy(dst, dst, sems, to).wait_recv()

    barrier = pltpu.get_barrier_semaphore()
    peers = [along(y, z, 1 - core)]
    peers += [along(y, (z + o) % nz, core) for o in range(1, nz)]
    peers += [along((y + o) % ny, z, core) for o in range(1, ny)]
    peers += [{"ch": (ch + o) % nch} for o in range(1, nch)]
    for peer in peers:
        pl.semaphore_signal(barrier, inc=1, device_id=peer, device_id_type=pl.DeviceIdType.MESH)
    has_next = jnp.logical_and(core == 1, ctx < last_ctx)
    has_before = jnp.logical_and(core == 0, ctx > 0)

    @pl.when(has_next)
    def _():
        pl.semaphore_signal(
            barrier, inc=1, device_id={"ctx": ctx + 1}, device_id_type=pl.DeviceIdType.MESH
        )

    @pl.when(has_before)
    def _():
        pl.semaphore_signal(
            barrier, inc=1, device_id={"ctx": ctx - 1}, device_id_type=pl.DeviceIdType.MESH
        )

    def rows_of(slot):
        return pl.ds(pl.multiple_of(slot * piece, piece), piece)

    def part_of(slot, part):
        return pl.ds(pl.multiple_of(slot * piece + part * (piece // 2), piece // 2), piece // 2)

    loads = [
        pltpu.make_async_copy(
            w_ref.at[i], weights.at[rows_of(ctx), pl.ds(i * width, width)], load_sem.at[i]
        )
        for i in range(3)
    ]
    loads.append(pltpu.make_async_copy(emb_ref.at[pl.ds(64, 32)], emb, load_sem.at[3]))
    loads.append(pltpu.make_async_copy(table_ref.at[:, pl.ds(64, 32)], table, load_sem.at[4]))
    for load in loads:
        load.start()
    tok_ref[...] = jnp.broadcast_to(token_ref[...], tok_ref.shape)

    def slot(yy, zz, cc):
        return (yy * nz + zz) * 2 + cc

    def event_of(e):
        if e == 0:
            return z, None
        r = (e - 1) // 2
        if e % 2 == 1:
            return z - 1 - r, lambda: z - 1 - r >= 0
        return z + 1 + r, lambda: z + 1 + r < nz

    def guarded(cond, body):
        if cond is None:
            body()
        else:
            pl.when(cond())(body)

    up, down = (y + 1) % ny, (y + ny - 1) % ny

    def pair(e, kind, rows, cond):
        def make():
            view = weights.at[rows()]
            return view, view, sems_of(pair_sem, e, kind), along(y, z, 1 - core)

        send(make, cond)

    def y_sends(e, zz, cond):
        if ny > 1:
            for way, to in ((0, up), (1, down)):

                def make(way=way, to=to):
                    view = weights.at[rows_of(slot(y, zz, core))]
                    return view, view, sems_of(y_sem, e, way), along(to, z, core)

                send(make, cond)

    def z_send(way, hop, zz, cond):
        def inside():
            return z + 1 < nz if way == 0 else z > 0

        def wanted():
            return inside() if cond is None else jnp.logical_and(cond(), inside())

        def make():
            view = weights.at[rows_of(slot(y, zz, core))]
            to = z + 1 if way == 0 else z - 1
            return view, view, sems_of(z_sem, hop, way), along(y, to, core)

        pl.when(inside())(lambda: send(make, wanted))

    def own_weights():
        if nz > 1:
            z_send(0, 0, z, None)
            z_send(1, 0, z, None)
        y_sends(0, z, None)
        pair(0, 0, lambda: rows_of(slot(y, z, core)), None)

    def z_forward(r):
        for way in (0, 1):
            e = 1 + 2 * r + way
            zz, valid = event_of(e)

            def body(way=way, e=e, zz=zz, valid=valid):
                rows = rows_of(slot(y, zz, core))
                arrived(
                    weights.at[rows],
                    (z_sem.at[0, r, way], z_sem.at[1, r, way]),
                    along(y, zz, core),
                )
                if r + 1 < nz - 1:
                    z_send(way, r + 1, zz, valid)

            guarded(valid, body)

    def z_spread(r):
        for way in (0, 1):
            e = 1 + 2 * r + way
            zz, valid = event_of(e)

            def body(e=e, zz=zz, valid=valid):
                y_sends(e, zz, valid)
                pair(e, 0, lambda: rows_of(slot(y, zz, core)), valid)

            guarded(valid, body)

    def z_round(r):
        z_forward(r)
        z_spread(r)

    def y_first(e):
        zz, valid = event_of(e)

        def body():
            for way, origin, to in ((0, down, up), (1, up, down)):
                rows = rows_of(slot(origin, zz, core))
                arrived(
                    weights.at[rows],
                    (y_sem.at[0, e, way], y_sem.at[1, e, way]),
                    along(origin, z, core),
                )

                def make(way=way, origin=origin, to=to):
                    view = weights.at[part_of(slot(origin, zz, core), way)]
                    return view, view, sems_of(y_sem, e, 2 + way), along(to, z, core)

                send(make, valid)
                pair(e, 1 + way, lambda origin=origin: rows_of(slot(origin, zz, core)), valid)

        if ny > 1:
            guarded(valid, body)

    def y_second(e):
        zz, valid = event_of(e)

        def body():
            for way, origin in ((0, down), (1, up)):
                half = part_of(slot((y + 2) % ny, zz, core), way)
                arrived(
                    weights.at[half],
                    (y_sem.at[0, e, 2 + way], y_sem.at[1, e, 2 + way]),
                    along(origin, z, core),
                )
                pair(
                    e, 3 + way, lambda way=way: part_of(slot((y + 2) % ny, zz, core), way), valid
                )

        if ny > 1:
            guarded(valid, body)

    def pair_in(e, kinds):
        zz, valid = event_of(e)

        def body():
            other = along(y, z, 1 - core)

            def one(kind, rows):
                if kind in kinds:
                    arrived(weights.at[rows], sems_of(pair_sem, e, kind), other)

            one(0, rows_of(slot(y, zz, 1 - core)))
            if ny > 1:
                one(1, rows_of(slot(down, zz, 1 - core)))
                one(2, rows_of(slot(up, zz, 1 - core)))
                one(3, part_of(slot((y + 2) % ny, zz, 1 - core), 0))
                one(4, part_of(slot((y + 2) % ny, zz, 1 - core), 1))

        guarded(valid, body)

    events = list(range(1 + 2 * (nz - 1)))

    group_row = (group_ref[...] - ch * (width // 16)).astype(F32)
    of_group = (
        lax.broadcasted_iota(jnp.int32, (32, width), 0).astype(F32) == group_row
    ).astype(F32)
    rate_in = rate_ref[...]
    twice = 2.0 * rate_in
    series = jnp.ones_like(twice)
    for k in range(9, 1, -1):
        series = 1.0 - twice * (1.0 / k) * series
    both = jnp.concatenate([rate_in, residue_ref[...] * jnp.sqrt(twice * series)], axis=0)
    chan[...] = jnp.dot(
        both, of_group, precision=lax.Precision.HIGHEST, preferred_element_type=F32
    )

    def one_hots(joined, count):
        codes = 64 + lax.broadcasted_iota(jnp.int32, (32, count), 0)
        for back in range(3):
            shifted = joined if back == 0 else pltpu.roll(joined, back, 1)
            row = shifted[0:1, 128:]
            hot[back, 0:count] = (row == codes).astype(F32).T.astype(BF16)

    def streams(rows):
        for tile in range(width // 128):
            cols = pl.ds(tile * 128, 128)

            def mixed(i, cols=cols):
                total = None
                for back in range(3):
                    picked = jnp.dot(
                        hot[back, 0:rows], table[i, :, cols], preferred_element_type=F32
                    )
                    term = ltaps_ref[back, i : i + 1, cols] * picked
                    total = term if total is None else total + term
                return total

            key = mixed(1)
            prod[tile, 0:rows] = (key * mixed(2)).astype(BF16).astype(F32)
            query[0:rows, cols] = mixed(0)

    one_hots(jnp.concatenate([jnp.full((8, 128), -1, jnp.int32), tok_ref[...]], axis=1), tokens)
    loads[3].wait()
    loads[4].wait()
    resid[...] = jnp.dot(hot[0], emb[...], preferred_element_type=F32)
    streams(tokens)

    extra = jnp.logical_or(has_next, has_before)
    pl.semaphore_wait(barrier, len(peers) + extra.astype(jnp.int32))
    tail_tok = pl.ds(tokens - 128, 128)

    @pl.when(ctx < last_ctx)
    def _():
        send(
            lambda: (tok_ref.at[:, tail_tok], halo_tok, sems_of(tok_sem), {"ctx": ctx + 1}),
            lambda: ctx < last_ctx,
        )

    for load in loads[:3]:
        load.wait()
    own_weights()

    taps = filt_ref.shape[1]

    def make_toep(g, carry):
        line = filt_ref[pl.ds(g, 1), :]
        line = jnp.concatenate([line, jnp.zeros((1, taps), F32)], axis=1)
        spread = jnp.broadcast_to(line, (2 * taps, 2 * taps))
        turned_line = pltpu.roll(spread, taps, 1, stride=1, stride_axis=0)
        toep[g] = turned_line[:, :taps].astype(BF16)
        return carry

    lax.fori_loop(0, filt_ref.shape[0], make_toep, 0)
    lanes = lax.broadcasted_iota(jnp.int32, (128, width), 1)
    rank = jnp.zeros((1, width), F32)
    group_col = jnp.broadcast_to(group_row, (128, width)).T
    for tile in range(width // 128):
        mine = group_col[tile * 128 : (tile + 1) * 128, 0:1]
        above = tile * 128 + lax.broadcasted_iota(jnp.int32, (128, width), 0) < lanes
        same = jnp.logical_and(mine == group_row, above)
        rank = rank + jnp.sum(same.astype(F32), axis=0, keepdims=True)
    placed = group_row * float(width // 32) + rank
    for tile in range(width // 128):
        place = (tile * 128 + lax.broadcasted_iota(jnp.int32, (128, width), 0)).astype(F32)
        perm[tile * 128 : (tile + 1) * 128, :] = (place == placed).astype(F32).astype(BF16)

    @pl.when(ctx > 0)
    def _():
        arrived(halo_tok, (tok_sem.at[0], tok_sem.at[1]), {"ctx": ctx - 1})
        one_hots(jnp.concatenate([halo_tok[...], tok_ref[:, 0:128]], axis=1), 128)
        streams(16)

    chunk = tokens // 8
    chunk_id = lax.broadcasted_iota(jnp.int32, (8, 128), 0)

    def row_b(ref, p, cols):
        return jnp.broadcast_to(ref[p : p + 1, cols], (8, 128))

    for tile in range(width // 128):
        cols = pl.ds(tile * 128, 128)
        decay = [jnp.exp(-row_b(chan, p, cols)) for p in range(16)]

        def step(k, states, tile=tile, decay=decay):
            row = prod[tile, pl.ds(k, 8, stride=chunk), :]
            return tuple(d * s + row for d, s in zip(decay, states))

        states = lax.fori_loop(
            0, chunk, step, tuple(jnp.zeros((8, 128), F32) for _ in range(16)), unroll=4
        )
        for p in range(16):
            rate = row_b(chan, p, cols) * float(chunk)
            total = states[p]
            for by in (1, 2, 4):
                moved = jnp.exp(-rate * float(by)) * pltpu.roll(total, by, 0)
                total = total + jnp.where(chunk_id >= by, moved, 0.0)
            end_own[p : p + 1, cols] = total[7:8]
            excl[p, :, cols] = jnp.where(chunk_id >= 1, pltpu.roll(total, 1, 0), 0.0)

    def own_conv(tiles):
        for tile in tiles:
            cols = pl.ds(tile * 128, 128)
            decay = [jnp.exp(-row_b(chan, p, cols)) for p in range(16)]
            weigh = [row_b(chan, 16 + p, cols) for p in range(16)]

            def step2(k, states, tile=tile, decay=decay, weigh=weigh):
                where = pl.ds(k, 8, stride=chunk)
                row = prod[tile, where, :]
                states = tuple(d * s + row for d, s in zip(decay, states))
                sums = [None] * 4
                for p in range(16):
                    term = weigh[p] * states[p]
                    sums[p % 4] = term if sums[p % 4] is None else sums[p % 4] + term
                conv[tile, where, :] = (sums[0] + sums[1]) + (sums[2] + sums[3])
                return states

            start = tuple(excl[p, :, cols] for p in range(16))
            lax.fori_loop(0, chunk, step2, start, unroll=2)

    rates = chan[0:16, :]
    send(lambda: (end_own, end_other, sems_of(end_sem), along(y, z, 1 - core)))
    arrived(end_other, (end_sem.at[0], end_sem.at[1]), along(y, z, 1 - core))
    first = jnp.where(core == 0, end_own[...], end_other[...])
    second = jnp.where(core == 0, end_other[...], end_own[...])
    decay_dev = jnp.exp(-rates * float(tokens))
    chip_own[...] = first * decay_dev + second
    for o in range(1, nz):
        send(
            lambda o=o: (
                chip_own,
                chip_all.at[z],
                (chip_sem.at[0, (z + o) % nz], chip_sem.at[1, z]),
                along(y, (z + o) % nz, core),
            )
        )
    own_conv((0, 1))
    if nz > 1:
        z_forward(0)
    for o in range(1, nz):
        origin = (z + nz - o) % nz
        arrived(
            chip_all.at[origin], (chip_sem.at[0, z], chip_sem.at[1, origin]), along(y, origin, core)
        )
    decay_chip = jnp.exp(-rates * float(2 * tokens))
    whole = None
    for zz in range(nz):
        if nz == 1:
            this = chip_own[...]
        else:
            this = jnp.where(z == zz, chip_own[...], chip_all[zz])
        whole = this if whole is None else whole * decay_chip + this
    row_own[...] = whole
    for o in range(1, ny):

        @pl.when(y + o < ny)
        def _(o=o):
            send(
                lambda: (
                    row_own,
                    row_all.at[y],
                    (row_sem.at[0, (y + o) % ny], row_sem.at[1, y]),
                    along((y + o) % ny, z, core),
                ),
                lambda: y + o < ny,
            )

    if nz > 1:
        z_spread(0)
    y_first(0)
    own_conv((2, 3))
    for o in range(1, ny):

        @pl.when(y >= o)
        def _(o=o):
            origin = (y + ny - o) % ny
            arrived(
                row_all.at[origin],
                (row_sem.at[0, y], row_sem.at[1, origin]),
                along(origin, z, core),
            )

    decay_row = jnp.exp(-rates * float(2 * tokens * nz))
    carried = jnp.zeros((16, width), F32)
    for yy in range(ny - 1):
        carried = jnp.where(yy < y, carried * decay_row + row_all[yy], carried)
    for zz in range(nz - 1):
        carried = jnp.where(zz < z, carried * decay_chip + chip_all[zz], carried)
    carried = jnp.where(core == 1, carried * decay_dev + first, carried)
    end_other[...] = carried

    for tile in range(width // 128):
        cols = pl.ds(tile * 128, 128)
        start = []
        for p in range(16):
            rate = row_b(chan, p, cols)
            since = rate * (chunk_id * chunk + 1).astype(F32)
            start.append(row_b(chan, 16 + p, cols) * row_b(end_other, p, cols) * jnp.exp(-since))
        decay = [jnp.exp(-row_b(chan, p, cols)) for p in range(16)]

        def step3(k, states, tile=tile, decay=decay):
            where = pl.ds(k, 8, stride=chunk)
            sums = list(states[:4])
            for p in range(4, 16):
                sums[p % 4] = sums[p % 4] + states[p]
            conv[tile, where, :] += (sums[0] + sums[1]) + (sums[2] + sums[3])
            return tuple(d * s for d, s in zip(decay, states))

        lax.fori_loop(0, chunk, step3, tuple(start), unroll=4)

    squares = None
    for tile in range(width // 128):
        cols = pl.ds(tile * 128, 128)
        whole = conv[tile] + lskip_ref[:, cols] * prod[tile]
        middle = (resid[:, cols] + query[:, cols] * whole).astype(BF16)
        feats[ch, :, cols] = middle
        wide = middle.astype(F32)
        resid[:, cols] = wide
        squares = wide * wide if squares is None else squares + wide * wide
    note_own[...] = jnp.broadcast_to(jnp.sum(squares.T, axis=0, keepdims=True), note_own.shape)
    note_own[1:2, :] = gain_ref[...].astype(F32)
    for o in range(1, nch):
        send(
            lambda o=o: (
                note_own,
                note_all.at[ch],
                (note_sem.at[0, (ch + o) % nch], note_sem.at[1, ch]),
                {"ch": (ch + o) % nch},
            )
        )

    right, left = (x + 1) % nx, (x + nx - 1) % nx
    far_parts = 4
    far_rows = tokens // far_parts

    def rows_x(e):
        return (0, tokens) if e == 0 else ((e - 1) * far_rows, far_rows)

    def half_x(e, way):
        base, count = rows_x(e)
        return pl.ds(base + way * (count // 2), count // 2)

    def x_sends(e):
        if nx > 1:
            for way, to in ((0, right), (1, left)):

                def make(way=way, to=to):
                    view = feats.at[side(e) * nx + x, pl.ds(*rows_x(e))]
                    return view, view, sems_of(x_sem, e, way), across(h, to)

                send(make)

    def side(e):
        return h if e == 0 else 1 - h

    def x_first(e):
        if nx > 1:
            for way, origin, to in ((0, left, right), (1, right, left)):
                block = side(e) * nx + origin
                arrived(
                    feats.at[block, pl.ds(*rows_x(e))], sems_of(x_sem, e, way), across(h, origin)
                )

                def make(way=way, block=block, to=to):
                    part = feats.at[block, half_x(e, way)]
                    return part, part, sems_of(x_sem, e, 2 + way), across(h, to)

                send(make)

    def x_second(e):
        if nx > 1:
            for way, origin in ((0, left), (1, right)):
                part = feats.at[side(e) * nx + (x + 2) % nx, half_x(e, way)]
                arrived(part, sems_of(x_sem, e, 2 + way), across(h, origin))

    def far_in(k):
        if nh > 1:
            part = feats.at[(1 - h) * nx + x, pl.ds(k * far_rows, far_rows)]
            arrived(part, sems_of(far_sem, k), across(1 - h, x))
            x_sends(1 + k)

    def x_far_first(k):
        if nh > 1:
            x_first(1 + k)

    x_sends(0)
    def far_out(*which):
        if nh > 1:
            for k in which:

                def make(k=k):
                    part = feats.at[ch, pl.ds(k * far_rows, far_rows)]
                    return part, part, sems_of(far_sem, k), across(1 - h, x)

                send(make)

    if nz > 2:
        z_round(1)

    def y_first_if(*which):
        for e in which:
            if e in events:
                y_first(e)

    def y_second_if(*which):
        for e in which:
            if e in events:
                y_second(e)

    acc[...] = jnp.zeros_like(acc)
    y_first_if(1)
    x_first(0)
    if nz > 3:
        z_round(2)
    far_out(*range(far_parts))
    y_first_if(2)
    far_in(0)
    y_first_if(3, 4)
    far_in(1)
    x_far_first(0)
    y_second(0)
    far_in(2)
    x_far_first(1)
    far_in(3)
    y_first_if(5, 6)

    for o in range(1, nch):
        origin = (ch + nch - o) % nch
        arrived(
            note_all.at[origin], (note_sem.at[0, ch], note_sem.at[1, origin]), {"ch": origin}
        )
    note_all[ch] = note_own[...]
    total = note_all[0, 0:1, :]
    for o in range(1, nch):
        total = total + note_all[o, 0:1, :]
    factor = lax.rsqrt(total / float(width * nch) + EPSILON)
    scale[...] = jnp.broadcast_to(factor, (128, tokens)).T

    per_tile = 256
    per_row = nch // ny
    wide_all = acc.shape[1]

    def block_product(block, top, count):
        gain = note_all[block, 1:2, :]
        for tile in range(width // 128):
            cols = pl.ds(tile * 128, 128)
            wide = feats[block, top : top + count, cols].astype(F32) * scale[top : top + count, :]
            half_norm[top : top + count, cols] = (
                wide * gain[:, tile * 128 : (tile + 1) * 128]
            ).astype(BF16)
        rows = pl.ds(pl.multiple_of(block * width, width), width)
        for tile in range(wide_all // per_tile):
            cols = pl.ds(tile * per_tile, per_tile)
            acc[HALO + top : HALO + top + count, cols] += jnp.dot(
                half_norm[top : top + count, :], weights[rows, cols], preferred_element_type=F32
            )

    def early(block):
        same = block // nx == h
        if ny == 1:
            return same
        return jnp.logical_and(same, block // per_row != (y + 2) % ny)

    def late(block):
        return jnp.logical_not(early(block))

    def product_if(wanted, first, count, top, rows):
        def body(i, carry):
            block = first + i

            @pl.when(wanted(block))
            def _():
                block_product(block, top, rows)

            return carry

        lax.fori_loop(0, count, body, 0)

    split = nch > 1
    x_second(0)
    x_far_first(2)
    for e in events:
        pair_in(e, (0, 1, 2))
    if split:
        product_if(early, h * nx, nx // 2, 0, tokens)
    x_far_first(3)
    y_second_if(1, 2)
    if split:
        product_if(early, h * nx + nx // 2, nx // 2, 0, tokens)
    y_second_if(3, 4, 5, 6)
    if nh > 1:
        for k in range(far_parts):
            x_second(1 + k)
    for e in events:
        pair_in(e, (3, 4))

    body_rows = tokens - HALO
    if split:
        product_if(late, 0, nch, body_rows, HALO)
    else:
        block_product(0, body_rows, HALO)
    for tile in range(wide_all // 256):
        cols = pl.ds(tile * 256, 256)
        last = acc[tokens:, cols].astype(BF16)
        tail_out[:, cols] = last
        acc[tokens:, cols] = last.astype(F32)
    tail_parts = (
        (pl.ds(0, HALO), pl.ds(width, 2 * width)),
        (pl.ds(HALO - 16, 16), pl.ds(0, width)),
    )

    @pl.when(ctx < last_ctx)
    def _():
        for k, part in enumerate(tail_parts):
            send(
                lambda k=k, part=part: (
                    tail_out.at[part],
                    tail_in.at[part],
                    sems_of(tail_sem, k),
                    {"ctx": ctx + 1},
                ),
                lambda: ctx < last_ctx,
            )

    if split:
        product_if(late, 0, nch, 0, body_rows)
    else:
        block_product(0, 0, body_rows)
    for tile in range(wide_all // 256):
        cols = pl.ds(tile * 256, 256)
        acc[HALO:tokens, cols] = acc[HALO:tokens, cols].astype(BF16).astype(F32)

    def mixed2(i, base, count, tile):
        cols = pl.ds(i * width + tile * 128, 128)
        at = pl.ds(tile * 128, 128)
        total = None
        for back in range(3):
            term = (
                mtaps_ref[back, i : i + 1, at]
                * acc[base - back : base - back + count, cols]
            )
            total = term if total is None else total + term
        return total

    members = width // 32
    flip = (((0,), (0,)), ((), ()))

    def products(bases):
        for tile in range(width // 128):
            cols = pl.ds(tile * 128, 128)
            for base in bases:
                made = mixed2(1, base, 128, tile) * mixed2(2, base, 128, tile)
                prod2[base - HALO + 128 : base - HALO + 256, cols] = made.astype(BF16)
                if base >= HALO:
                    query[base - HALO : base - HALO + 128, cols] = mixed2(0, base, 128, tile)
        top, end = bases[0] - HALO + 128, bases[-1] - HALO + 256
        for tile in range(width // 128):
            lines = pl.ds(tile * 128, 128)
            made = lax.dot_general(
                perm[lines, :],
                prod2[top:end, :],
                (((1,), (1,)), ((), ())),
                preferred_element_type=F32,
            )
            turned[lines, top:end] = made.astype(BF16)

    def filtered(blocks):
        def one_group(g, carry):
            lines = pl.ds(pl.multiple_of(g * members, members), members)
            data = jnp.concatenate(
                [turned[lines, n * 128 : n * 128 + 256] for n in blocks], axis=0
            )
            made = jnp.dot(data, toep[g], preferred_element_type=F32)
            upper = made.astype(BF16)
            lower = (made - upper.astype(F32)).astype(BF16)
            for k, n in enumerate(blocks):
                conv_hi[lines, n * 128 : (n + 1) * 128] = upper[k * members : (k + 1) * members]
                conv_lo[lines, n * 128 : (n + 1) * 128] = lower[k * members : (k + 1) * members]
            return carry

        lax.fori_loop(0, 32, one_group, 0, unroll=4)
        top, end = blocks[0] * 128, (blocks[-1] + 1) * 128
        for tile in range(width // 256):
            cols = pl.ds(tile * 256, 256)
            made = lax.dot_general(
                conv_hi[:, top:end], perm[:, cols], flip, preferred_element_type=F32
            )
            made = made + lax.dot_general(
                conv_lo[:, top:end], perm[:, cols], flip, preferred_element_type=F32
            )
            made = made + mskip_ref[:, cols] * prod2[128 + top : 128 + end, cols].astype(F32)
            out_ref[top:end, cols] = (
                resid[top:end, cols] + query[top:end, cols] * made
            ).astype(BF16)

    def put(part):
        rows = pl.ds(part * (tokens // 2), tokens // 2)
        return pltpu.make_async_copy(out_ref.at[rows], out_hbm.at[rows], out_sem.at[part])

    products([HALO + 128, HALO + 256, HALO + 384])
    filtered((2, 3))
    put(1).start()
    for make, cond in waits:
        if cond is None:
            copy(*make()).wait_send()
        else:
            pl.when(cond())(lambda make=make: copy(*make()).wait_send())

    @pl.when(ctx > 0)
    def _():
        for k, part in enumerate(tail_parts):
            arrived(tail_in.at[part], sems_of(tail_sem, k), {"ctx": ctx - 1})
        acc[0:HALO, width:] = tail_in[:, width:].astype(F32)
        acc[HALO - 16 : HALO, 0:width] = tail_in[HALO - 16 :, 0:width].astype(F32)

    products([HALO - 128, HALO])
    filtered((0, 1))
    put(0).start()
    put(0).wait()
    put(1).wait()


def local(sizes, *arrays):
    (
        token_ids,
        embedding,
        long_table,
        long_taps,
        long_residue,
        long_rate,
        long_skip,
        medium_gain,
        medium_weight,
        medium_taps,
        medium_group_filter,
        medium_skip,
        filter_group,
    ) = arrays
    ny, nz, nh, nx = sizes
    nch, nctx = nh * nx, 2 * ny * nz
    tokens, width = token_ids.shape[0], embedding.shape[1]
    piece = medium_weight.shape[0]
    events = 1 + 2 * (nz - 1)
    hops = max(nz - 1, 1)
    vmem = pl.BlockSpec(memory_space=pltpu.VMEM)
    hbm = pl.BlockSpec(memory_space=pl.ANY)
    dma = pltpu.SemaphoreType.DMA
    return pl.pallas_call(
        functools.partial(kernel, sizes),
        out_shape=jax.ShapeDtypeStruct((tokens, width), BF16),
        in_specs=[vmem, hbm, hbm] + [vmem] * 5 + [hbm] + [vmem] * 4,
        out_specs=hbm,
        scratch_shapes=[
            pltpu.VMEM((tokens, width), BF16),
            pltpu.VMEM((32, width), BF16),
            pltpu.VMEM((3, 32, width), BF16),
            pltpu.VMEM((8, tokens), jnp.int32),
            pltpu.VMEM((nctx * piece, 3 * width), BF16),
            pltpu.VMEM((nch, tokens, width), BF16),
            pltpu.VMEM((HALO + tokens, 3 * width), F32),
            pltpu.VMEM((3, tokens, 32), BF16),
            pltpu.VMEM((8, 128), jnp.int32),
            pltpu.VMEM((width // 128, tokens, 128), F32),
            pltpu.VMEM((tokens, width), F32),
            pltpu.VMEM((tokens, width), F32),
            pltpu.VMEM((width // 128, tokens, 128), F32),
            pltpu.VMEM((32, width), F32),
            pltpu.VMEM((16, 8, width), F32),
            pltpu.VMEM((16, width), F32),
            pltpu.VMEM((16, width), F32),
            pltpu.VMEM((16, width), F32),
            pltpu.VMEM((nz, 16, width), F32),
            pltpu.VMEM((16, width), F32),
            pltpu.VMEM((ny, 16, width), F32),
            pltpu.VMEM((8, tokens), F32),
            pltpu.VMEM((nch, 8, tokens), F32),
            pltpu.VMEM((tokens, 128), F32),
            pltpu.VMEM((tokens, width), BF16),
            pltpu.VMEM((width, width), BF16),
            pltpu.VMEM((32, 256, 128), BF16),
            pltpu.VMEM((HALO, 3 * width), BF16),
            pltpu.VMEM((HALO, 3 * width), BF16),
            pltpu.VMEM((128 + tokens, width), BF16),
            pltpu.VMEM((width, 128 + tokens), BF16),
            pltpu.VMEM((width, tokens), BF16),
            pltpu.VMEM((width, tokens), BF16),
            dma((5,)),
            dma((2,)),
            dma((2, hops, 2)),
            dma((2, events, 4)),
            dma((2, events, 5)),
            dma((2,)),
            dma((2, nz)),
            dma((2, ny)),
            dma((2, nch)),
            dma((2, 5, 4)),
            dma((2, 4)),
            dma((2, 2)),
            dma((2,)),
        ],
        compiler_params=pltpu.CompilerParams(
            collective_id=0, has_side_effects=True, vmem_limit_bytes=60 << 20
        ),
    )(
        token_ids[None],
        embedding,
        jnp.transpose(long_table, (1, 0, 2)),
        long_taps,
        long_residue.T,
        long_rate.T,
        long_skip[None],
        medium_gain[None],
        jnp.transpose(medium_weight, (1, 0, 2)),
        medium_taps,
        medium_group_filter,
        medium_skip[None],
        filter_group[None],
    )


def solution(mesh, sizes=(4, 4, 2, 4)):
    in_specs = (
        P("ctx"),
        P(None, "ch"),
        P(None, None, "ch"),
        P(None, None, "ch"),
        P("ch", None),
        P("ch", None),
        P("ch"),
        P("ch"),
        P("ctx", None, "ch"),
        P(None, None, "ch"),
        P("ch", None),
        P("ch"),
        P("ch"),
    )
    return jax.shard_map(
        functools.partial(local, sizes),
        mesh=mesh,
        in_specs=in_specs,
        out_specs=P("ctx", "ch"),
        check_vma=False,
    )
```

```python
import functools

import jax
import jax.numpy as jnp
from jax import lax
from jax.experimental import pallas as pl
from jax.experimental.pallas import tpu as pltpu
from jax.sharding import PartitionSpec as P

EPSILON = 1e-06
HALO = 144
F32 = jnp.float32
BF16 = jnp.bfloat16


def kernel(
    sizes,
    token_ref,
    emb_ref,
    table_ref,
    ltaps_ref,
    residue_ref,
    rate_ref,
    lskip_ref,
    gain_ref,
    w_ref,
    mtaps_ref,
    filt_ref,
    mskip_ref,
    group_ref,
    out_hbm,
    out_ref,
    emb,
    table,
    tok_ref,
    weights,
    feats,
    acc,
    hot,
    halo_tok,
    prod,
    query,
    resid,
    conv,
    chan,
    excl,
    end_own,
    end_other,
    chip_own,
    chip_all,
    row_own,
    row_all,
    note_own,
    note_all,
    scale,
    half_norm,
    perm,
    toep,
    tail_out,
    tail_in,
    prod2,
    turned,
    conv_hi,
    load_sem,
    tok_sem,
    z_sem,
    y_sem,
    pair_sem,
    end_sem,
    chip_sem,
    row_sem,
    note_sem,
    x_sem,
    far_sem,
    tail_sem,
    out_sem,
):
    ny, nz, nh, nx = sizes
    nch = nh * nx
    tokens, width = query.shape
    piece = w_ref.shape[1]
    ctx, ch = lax.axis_index("ctx"), lax.axis_index("ch")
    core, chip = ctx % 2, ctx // 2
    z, y = chip % nz, chip // nz
    x, h = ch % nx, ch // nx
    last_ctx = 2 * ny * nz - 1
    waits = []

    def along(yy, zz, cc):
        return {"ctx": (yy * nz + zz) * 2 + cc}

    def across(hh, xx):
        return {"ch": hh * nx + xx}

    def copy(src, dst, sems, to):
        made = pltpu.make_async_remote_copy(
            src_ref=src,
            dst_ref=dst,
            send_sem=sems[0],
            recv_sem=sems[1],
            device_id=to,
            device_id_type=pl.DeviceIdType.MESH,
        )
        return made

    def send(make, cond=None):
        copy(*make()).start()
        waits.append((make, cond))

    def sems_of(ref, *index):
        return ref.at[(0, *index)], ref.at[(1, *index)]

    def arrived(dst, sems, to):
        copy(dst, dst, sems, to).wait_recv()

    barrier = pltpu.get_barrier_semaphore()
    peers = [along(y, z, 1 - core)]
    peers += [along(y, (z + o) % nz, core) for o in range(1, nz)]
    peers += [along((y + o) % ny, z, core) for o in range(1, ny)]
    peers += [{"ch": (ch + o) % nch} for o in range(1, nch)]
    for peer in peers:
        pl.semaphore_signal(barrier, inc=1, device_id=peer, device_id_type=pl.DeviceIdType.MESH)
    has_next = jnp.logical_and(core == 1, ctx < last_ctx)
    has_before = jnp.logical_and(core == 0, ctx > 0)

    @pl.when(has_next)
    def _():
        pl.semaphore_signal(
            barrier, inc=1, device_id={"ctx": ctx + 1}, device_id_type=pl.DeviceIdType.MESH
        )

    @pl.when(has_before)
    def _():
        pl.semaphore_signal(
            barrier, inc=1, device_id={"ctx": ctx - 1}, device_id_type=pl.DeviceIdType.MESH
        )

    def rows_of(slot):
        return pl.ds(pl.multiple_of(slot * piece, piece), piece)

    def part_of(slot, part):
        return pl.ds(pl.multiple_of(slot * piece + part * (piece // 2), piece // 2), piece // 2)

    loads = [
        pltpu.make_async_copy(
            w_ref.at[i], weights.at[rows_of(ctx), pl.ds(i * width, width)], load_sem.at[i]
        )
        for i in range(3)
    ]
    loads.append(pltpu.make_async_copy(emb_ref.at[pl.ds(64, 32)], emb, load_sem.at[3]))
    loads.append(pltpu.make_async_copy(table_ref.at[:, pl.ds(64, 32)], table, load_sem.at[4]))
    for load in loads:
        load.start()
    tok_ref[...] = jnp.broadcast_to(token_ref[...], tok_ref.shape)

    def slot(yy, zz, cc):
        return (yy * nz + zz) * 2 + cc

    def event_of(e):
        if e == 0:
            return z, None
        r = (e - 1) // 2
        if e % 2 == 1:
            return z - 1 - r, lambda: z - 1 - r >= 0
        return z + 1 + r, lambda: z + 1 + r < nz

    def guarded(cond, body):
        if cond is None:
            body()
        else:
            pl.when(cond())(body)

    up, down = (y + 1) % ny, (y + ny - 1) % ny

    def pair(e, kind, rows, cond):
        def make():
            view = weights.at[rows()]
            return view, view, sems_of(pair_sem, event_of(e)[0], kind), along(y, z, 1 - core)

        send(make, cond)

    def y_sends(e, zz, cond):
        if ny > 1:
            for way, to in ((0, up), (1, down)):

                def make(way=way, to=to):
                    view = weights.at[rows_of(slot(y, zz, core))]
                    return view, view, sems_of(y_sem, zz, way), along(to, z, core)

                send(make, cond)

    def z_send(way, hop, zz, cond):
        def inside():
            return z + 1 < nz if way == 0 else z > 0

        def wanted():
            return inside() if cond is None else jnp.logical_and(cond(), inside())

        def make():
            view = weights.at[rows_of(slot(y, zz, core))]
            to = z + 1 if way == 0 else z - 1
            return view, view, sems_of(z_sem, hop, way), along(y, to, core)

        pl.when(inside())(lambda: send(make, wanted))

    def own_weights():
        if nz > 1:
            z_send(0, 0, z, None)
            z_send(1, 0, z, None)
        y_sends(0, z, None)
        pair(0, 0, lambda: rows_of(slot(y, z, core)), None)

    def z_forward(r):
        for way in (0, 1):
            e = 1 + 2 * r + way
            zz, valid = event_of(e)

            def body(way=way, e=e, zz=zz, valid=valid):
                rows = rows_of(slot(y, zz, core))
                arrived(
                    weights.at[rows],
                    (z_sem.at[0, r, way], z_sem.at[1, r, way]),
                    along(y, zz, core),
                )
                if r + 1 < nz - 1:
                    z_send(way, r + 1, zz, valid)

            guarded(valid, body)

    def z_spread(r):
        for way in (0, 1):
            e = 1 + 2 * r + way
            zz, valid = event_of(e)

            def body(e=e, zz=zz, valid=valid):
                y_sends(e, zz, valid)
                pair(e, 0, lambda: rows_of(slot(y, zz, core)), valid)

            guarded(valid, body)

    def z_round(r):
        z_forward(r)
        z_spread(r)

    def y_first(e):
        zz, valid = event_of(e)

        def body():
            for way, origin, to in ((0, down, up), (1, up, down)):
                rows = rows_of(slot(origin, zz, core))
                arrived(
                    weights.at[rows],
                    sems_of(y_sem, zz, way),
                    along(origin, z, core),
                )

                def make(way=way, origin=origin, to=to):
                    view = weights.at[part_of(slot(origin, zz, core), way)]
                    return view, view, sems_of(y_sem, zz, 2 + way), along(to, z, core)

                send(make, valid)
                pair(e, 1 + way, lambda origin=origin: rows_of(slot(origin, zz, core)), valid)

        if ny > 1:
            guarded(valid, body)

    def y_second(e):
        zz, valid = event_of(e)

        def body():
            for way, origin in ((0, down), (1, up)):
                half = part_of(slot((y + 2) % ny, zz, core), way)
                arrived(
                    weights.at[half],
                    sems_of(y_sem, zz, 2 + way),
                    along(origin, z, core),
                )
                pair(
                    e, 3 + way, lambda way=way: part_of(slot((y + 2) % ny, zz, core), way), valid
                )

        if ny > 1:
            guarded(valid, body)

    def pair_in(e, kinds):
        zz, valid = event_of(e)

        def body():
            other = along(y, z, 1 - core)

            def one(kind, rows):
                if kind in kinds:
                    arrived(weights.at[rows], sems_of(pair_sem, zz, kind), other)

            one(0, rows_of(slot(y, zz, 1 - core)))
            if ny > 1:
                one(1, rows_of(slot(down, zz, 1 - core)))
                one(2, rows_of(slot(up, zz, 1 - core)))
                one(3, part_of(slot((y + 2) % ny, zz, 1 - core), 0))
                one(4, part_of(slot((y + 2) % ny, zz, 1 - core), 1))

        guarded(valid, body)

    events = list(range(1 + 2 * (nz - 1)))

    group_row = (group_ref[...] - ch * (width // 16)).astype(F32)
    of_group = (
        lax.broadcasted_iota(jnp.int32, (32, width), 0).astype(F32) == group_row
    ).astype(F32)
    rate_in = rate_ref[...]
    twice = 2.0 * rate_in
    series = jnp.ones_like(twice)
    for k in range(9, 1, -1):
        series = 1.0 - twice * (1.0 / k) * series
    both = jnp.concatenate([rate_in, residue_ref[...] * jnp.sqrt(twice * series)], axis=0)
    chan[...] = jnp.dot(
        both, of_group, precision=lax.Precision.HIGHEST, preferred_element_type=F32
    )

    def one_hots(joined, count):
        codes = 64 + lax.broadcasted_iota(jnp.int32, (32, count), 0)
        for back in range(3):
            shifted = joined if back == 0 else pltpu.roll(joined, back, 1)
            row = shifted[0:1, 128:]
            hot[back, 0:count] = (row == codes).astype(F32).T.astype(BF16)

    def streams(rows):
        for tile in range(width // 128):
            cols = pl.ds(tile * 128, 128)

            def mixed(i, cols=cols):
                total = None
                for back in range(3):
                    picked = jnp.dot(
                        hot[back, 0:rows], table[i, :, cols], preferred_element_type=F32
                    )
                    term = ltaps_ref[back, i : i + 1, cols] * picked
                    total = term if total is None else total + term
                return total

            key = mixed(1)
            prod[tile, 0:rows] = (key * mixed(2)).astype(BF16).astype(F32)
            query[0:rows, cols] = mixed(0)

    one_hots(jnp.concatenate([jnp.full((8, 128), -1, jnp.int32), tok_ref[...]], axis=1), tokens)
    loads[3].wait()
    loads[4].wait()
    resid[...] = jnp.dot(hot[0], emb[...], preferred_element_type=F32)
    streams(tokens)

    extra = jnp.logical_or(has_next, has_before)
    pl.semaphore_wait(barrier, len(peers) + extra.astype(jnp.int32))
    tail_tok = pl.ds(tokens - 128, 128)

    @pl.when(ctx < last_ctx)
    def _():
        send(
            lambda: (tok_ref.at[:, tail_tok], halo_tok, sems_of(tok_sem), {"ctx": ctx + 1}),
            lambda: ctx < last_ctx,
        )

    for load in loads[:3]:
        load.wait()
    own_weights()

    taps = filt_ref.shape[1]

    def make_toep(g, carry):
        line = filt_ref[pl.ds(g, 1), :]
        line = jnp.concatenate([line, jnp.zeros((1, taps), F32)], axis=1)
        spread = jnp.broadcast_to(line, (2 * taps, 2 * taps))
        turned_line = pltpu.roll(spread, taps, 1, stride=1, stride_axis=0)
        toep[g] = turned_line[:, :taps].astype(BF16)
        return carry

    lax.fori_loop(0, filt_ref.shape[0], make_toep, 0)
    lanes = lax.broadcasted_iota(jnp.int32, (128, width), 1)
    rank = jnp.zeros((1, width), F32)
    group_col = jnp.broadcast_to(group_row, (128, width)).T
    for tile in range(width // 128):
        mine = group_col[tile * 128 : (tile + 1) * 128, 0:1]
        above = tile * 128 + lax.broadcasted_iota(jnp.int32, (128, width), 0) < lanes
        same = jnp.logical_and(mine == group_row, above)
        rank = rank + jnp.sum(same.astype(F32), axis=0, keepdims=True)
    placed = group_row * float(width // 32) + rank
    for tile in range(width // 128):
        place = (tile * 128 + lax.broadcasted_iota(jnp.int32, (128, width), 0)).astype(F32)
        perm[tile * 128 : (tile + 1) * 128, :] = (place == placed).astype(F32).astype(BF16)

    @pl.when(ctx > 0)
    def _():
        arrived(halo_tok, (tok_sem.at[0], tok_sem.at[1]), {"ctx": ctx - 1})
        one_hots(jnp.concatenate([halo_tok[...], tok_ref[:, 0:128]], axis=1), 128)
        streams(16)

    chunk = tokens // 8
    chunk_id = lax.broadcasted_iota(jnp.int32, (8, 128), 0)

    def row_b(ref, p, cols):
        return jnp.broadcast_to(ref[p : p + 1, cols], (8, 128))

    for tile in range(width // 128):
        cols = pl.ds(tile * 128, 128)
        decay = [jnp.exp(-row_b(chan, p, cols)) for p in range(16)]

        def step(k, states, tile=tile, decay=decay):
            row = prod[tile, pl.ds(k, 8, stride=chunk), :]
            return tuple(d * s + row for d, s in zip(decay, states))

        states = lax.fori_loop(
            0, chunk, step, tuple(jnp.zeros((8, 128), F32) for _ in range(16)), unroll=4
        )
        for p in range(16):
            rate = row_b(chan, p, cols) * float(chunk)
            total = states[p]
            for by in (1, 2, 4):
                moved = jnp.exp(-rate * float(by)) * pltpu.roll(total, by, 0)
                total = total + jnp.where(chunk_id >= by, moved, 0.0)
            end_own[p : p + 1, cols] = total[7:8]
            excl[p, :, cols] = jnp.where(chunk_id >= 1, pltpu.roll(total, 1, 0), 0.0)

    def own_conv(tiles):
        for tile in tiles:
            cols = pl.ds(tile * 128, 128)
            decay = [jnp.exp(-row_b(chan, p, cols)) for p in range(16)]
            weigh = [row_b(chan, 16 + p, cols) for p in range(16)]

            def step2(k, states, tile=tile, decay=decay, weigh=weigh):
                where = pl.ds(k, 8, stride=chunk)
                row = prod[tile, where, :]
                states = tuple(d * s + row for d, s in zip(decay, states))
                sums = [None] * 4
                for p in range(16):
                    term = weigh[p] * states[p]
                    sums[p % 4] = term if sums[p % 4] is None else sums[p % 4] + term
                conv[tile, where, :] = (sums[0] + sums[1]) + (sums[2] + sums[3])
                return states

            start = tuple(excl[p, :, cols] for p in range(16))
            lax.fori_loop(0, chunk, step2, start, unroll=2)

    rates = chan[0:16, :]
    send(lambda: (end_own, end_other, sems_of(end_sem), along(y, z, 1 - core)))
    arrived(end_other, (end_sem.at[0], end_sem.at[1]), along(y, z, 1 - core))
    first = jnp.where(core == 0, end_own[...], end_other[...])
    second = jnp.where(core == 0, end_other[...], end_own[...])
    decay_dev = jnp.exp(-rates * float(tokens))
    chip_own[...] = first * decay_dev + second
    for o in range(1, nz):
        send(
            lambda o=o: (
                chip_own,
                chip_all.at[z],
                (chip_sem.at[0, (z + o) % nz], chip_sem.at[1, z]),
                along(y, (z + o) % nz, core),
            )
        )
    own_conv((0, 1))
    if nz > 1:
        z_forward(0)
    for o in range(1, nz):
        origin = (z + nz - o) % nz
        arrived(
            chip_all.at[origin], (chip_sem.at[0, z], chip_sem.at[1, origin]), along(y, origin, core)
        )
    decay_chip = jnp.exp(-rates * float(2 * tokens))
    whole = None
    for zz in range(nz):
        if nz == 1:
            this = chip_own[...]
        else:
            this = jnp.where(z == zz, chip_own[...], chip_all[zz])
        whole = this if whole is None else whole * decay_chip + this
    row_own[...] = whole
    for o in range(1, ny):

        @pl.when(y + o < ny)
        def _(o=o):
            send(
                lambda: (
                    row_own,
                    row_all.at[y],
                    (row_sem.at[0, (y + o) % ny], row_sem.at[1, y]),
                    along((y + o) % ny, z, core),
                ),
                lambda: y + o < ny,
            )

    if nz > 1:
        z_spread(0)
    y_first(0)
    own_conv((2, 3))
    for o in range(1, ny):

        @pl.when(y >= o)
        def _(o=o):
            origin = (y + ny - o) % ny
            arrived(
                row_all.at[origin],
                (row_sem.at[0, y], row_sem.at[1, origin]),
                along(origin, z, core),
            )

    decay_row = jnp.exp(-rates * float(2 * tokens * nz))
    carried = jnp.zeros((16, width), F32)
    for yy in range(ny - 1):
        carried = jnp.where(yy < y, carried * decay_row + row_all[yy], carried)
    for zz in range(nz - 1):
        carried = jnp.where(zz < z, carried * decay_chip + chip_all[zz], carried)
    carried = jnp.where(core == 1, carried * decay_dev + first, carried)
    end_other[...] = carried

    for tile in range(width // 128):
        cols = pl.ds(tile * 128, 128)
        start = []
        for p in range(16):
            rate = row_b(chan, p, cols)
            since = rate * (chunk_id * chunk + 1).astype(F32)
            start.append(row_b(chan, 16 + p, cols) * row_b(end_other, p, cols) * jnp.exp(-since))
        decay = [jnp.exp(-row_b(chan, p, cols)) for p in range(16)]

        def step3(k, states, tile=tile, decay=decay):
            where = pl.ds(k, 8, stride=chunk)
            sums = list(states[:4])
            for p in range(4, 16):
                sums[p % 4] = sums[p % 4] + states[p]
            conv[tile, where, :] += (sums[0] + sums[1]) + (sums[2] + sums[3])
            return tuple(d * s for d, s in zip(decay, states))

        lax.fori_loop(0, chunk, step3, tuple(start), unroll=4)

    squares = None
    for tile in range(width // 128):
        cols = pl.ds(tile * 128, 128)
        whole = conv[tile] + lskip_ref[:, cols] * prod[tile]
        middle = (resid[:, cols] + query[:, cols] * whole).astype(BF16)
        feats[ch, :, cols] = middle
        wide = middle.astype(F32)
        resid[:, cols] = wide
        squares = wide * wide if squares is None else squares + wide * wide
    note_own[...] = jnp.broadcast_to(jnp.sum(squares.T, axis=0, keepdims=True), note_own.shape)
    note_own[1:2, :] = gain_ref[...].astype(F32)
    for o in range(1, nch):
        send(
            lambda o=o: (
                note_own,
                note_all.at[ch],
                (note_sem.at[0, (ch + o) % nch], note_sem.at[1, ch]),
                {"ch": (ch + o) % nch},
            )
        )

    right, left = (x + 1) % nx, (x + nx - 1) % nx
    far_parts = 4
    far_rows = tokens // far_parts

    def rows_x(e):
        return (0, tokens) if e == 0 else ((e - 1) * far_rows, far_rows)

    def half_x(e, way):
        base, count = rows_x(e)
        return pl.ds(base + way * (count // 2), count // 2)

    def x_sends(e):
        if nx > 1:
            for way, to in ((0, right), (1, left)):

                def make(way=way, to=to):
                    view = feats.at[side(e) * nx + x, pl.ds(*rows_x(e))]
                    return view, view, sems_of(x_sem, e, way), across(h, to)

                send(make)

    def side(e):
        return h if e == 0 else 1 - h

    def x_first(e):
        if nx > 1:
            for way, origin, to in ((0, left, right), (1, right, left)):
                block = side(e) * nx + origin
                arrived(
                    feats.at[block, pl.ds(*rows_x(e))], sems_of(x_sem, e, way), across(h, origin)
                )

                def make(way=way, block=block, to=to):
                    part = feats.at[block, half_x(e, way)]
                    return part, part, sems_of(x_sem, e, 2 + way), across(h, to)

                send(make)

    def x_second(e):
        if nx > 1:
            for way, origin in ((0, left), (1, right)):
                part = feats.at[side(e) * nx + (x + 2) % nx, half_x(e, way)]
                arrived(part, sems_of(x_sem, e, 2 + way), across(h, origin))

    def far_in(k):
        if nh > 1:
            part = feats.at[(1 - h) * nx + x, pl.ds(k * far_rows, far_rows)]
            arrived(part, sems_of(far_sem, k), across(1 - h, x))
            x_sends(1 + k)

    def x_far_first(k):
        if nh > 1:
            x_first(1 + k)

    x_sends(0)
    def far_out(*which):
        if nh > 1:
            for k in which:

                def make(k=k):
                    part = feats.at[ch, pl.ds(k * far_rows, far_rows)]
                    return part, part, sems_of(far_sem, k), across(1 - h, x)

                send(make)

    if nz > 2:
        z_round(1)

    def y_first_if(*which):
        for e in which:
            if e in events:
                y_first(e)

    def y_second_if(*which):
        for e in which:
            if e in events:
                y_second(e)

    acc[...] = jnp.zeros_like(acc)
    y_first_if(1)
    x_first(0)
    if nz > 3:
        z_round(2)
    far_out(*range(far_parts))
    y_first_if(2)
    far_in(0)
    y_first_if(3, 4)
    far_in(1)
    x_far_first(0)
    y_second(0)
    far_in(2)
    x_far_first(1)
    far_in(3)
    y_first_if(5, 6)

    for o in range(1, nch):
        origin = (ch + nch - o) % nch
        arrived(
            note_all.at[origin], (note_sem.at[0, ch], note_sem.at[1, origin]), {"ch": origin}
        )
    note_all[ch] = note_own[...]
    total = note_all[0, 0:1, :]
    for o in range(1, nch):
        total = total + note_all[o, 0:1, :]
    factor = lax.rsqrt(total / float(width * nch) + EPSILON)
    scale[...] = jnp.broadcast_to(factor, (128, tokens)).T

    per_tile = 256
    per_row = nch // ny
    wide_all = acc.shape[1]

    def block_product(block, top, count):
        gain = note_all[block, 1:2, :]
        for tile in range(width // 128):
            cols = pl.ds(tile * 128, 128)
            wide = feats[block, top : top + count, cols].astype(F32) * scale[top : top + count, :]
            half_norm[top : top + count, cols] = (
                wide * gain[:, tile * 128 : (tile + 1) * 128]
            ).astype(BF16)
        rows = pl.ds(pl.multiple_of(block * width, width), width)
        for tile in range(wide_all // per_tile):
            cols = pl.ds(tile * per_tile, per_tile)
            acc[HALO + top : HALO + top + count, cols] += jnp.dot(
                half_norm[top : top + count, :], weights[rows, cols], preferred_element_type=F32
            )

    def early(block):
        same = block // nx == h
        if ny == 1:
            return same
        return jnp.logical_and(same, block // per_row != (y + 2) % ny)

    def late(block):
        return jnp.logical_not(early(block))

    def product_if(wanted, first, count, top, rows):
        def body(i, carry):
            block = first + i
            if wanted is None:
                block_product(block, top, rows)
            else:
                pl.when(wanted(block))(lambda: block_product(block, top, rows))
            return carry

        lax.fori_loop(0, count, body, 0)

    split = nch > 1
    x_second(0)
    x_far_first(2)
    y_second_if(1, 2, 3, 4)
    for e in events:
        pair_in(e, (0, 1, 2))
    if split:
        product_if(early, h * nx, nx // 2, 0, tokens)
    x_far_first(3)
    y_second_if(5, 6)
    if split:
        product_if(early, h * nx + nx // 2, nx // 2, 0, tokens)
    for e in events:
        pair_in(e, (3, 4))
    if split:
        product_if(late, h * nx, nx, 0, tokens)
    if nh > 1:
        for k in range(far_parts):
            x_second(1 + k)

    body_rows = tokens - HALO
    if split:
        product_if(None, (1 - h) * nx, nx, body_rows, HALO)
    else:
        block_product(0, body_rows, HALO)
    for tile in range(wide_all // 256):
        cols = pl.ds(tile * 256, 256)
        last = acc[tokens:, cols].astype(BF16)
        tail_out[:, cols] = last
        acc[tokens:, cols] = last.astype(F32)
    tail_parts = (
        (pl.ds(0, HALO), pl.ds(width, 2 * width)),
        (pl.ds(HALO - 16, 16), pl.ds(0, width)),
    )

    @pl.when(ctx < last_ctx)
    def _():
        for k, part in enumerate(tail_parts):
            send(
                lambda k=k, part=part: (
                    tail_out.at[part],
                    tail_in.at[part],
                    sems_of(tail_sem, k),
                    {"ctx": ctx + 1},
                ),
                lambda: ctx < last_ctx,
            )

    if split:
        product_if(None, (1 - h) * nx, nx, 0, body_rows)
    else:
        block_product(0, 0, body_rows)
    for tile in range(wide_all // 256):
        cols = pl.ds(tile * 256, 256)
        acc[HALO:tokens, cols] = acc[HALO:tokens, cols].astype(BF16).astype(F32)

    def mixed2(i, base, count, tile):
        cols = pl.ds(i * width + tile * 128, 128)
        at = pl.ds(tile * 128, 128)
        total = None
        for back in range(3):
            term = (
                mtaps_ref[back, i : i + 1, at]
                * acc[base - back : base - back + count, cols]
            )
            total = term if total is None else total + term
        return total

    members = width // 32
    flip = (((0,), (0,)), ((), ()))

    def products(bases):
        for tile in range(width // 128):
            cols = pl.ds(tile * 128, 128)
            for base in bases:
                made = mixed2(1, base, 128, tile) * mixed2(2, base, 128, tile)
                prod2[base - HALO + 128 : base - HALO + 256, cols] = made.astype(BF16)
                if base >= HALO:
                    query[base - HALO : base - HALO + 128, cols] = mixed2(0, base, 128, tile)
        top, end = bases[0] - HALO + 128, bases[-1] - HALO + 256
        for tile in range(width // 128):
            lines = pl.ds(tile * 128, 128)
            made = lax.dot_general(
                perm[lines, :],
                prod2[top:end, :],
                (((1,), (1,)), ((), ())),
                preferred_element_type=F32,
            )
            turned[lines, top:end] = made.astype(BF16)

    def filtered(blocks):
        def one_group(g, carry):
            lines = pl.ds(pl.multiple_of(g * members, members), members)
            data = jnp.concatenate(
                [turned[lines, n * 128 : n * 128 + 256] for n in blocks], axis=0
            )
            made = jnp.dot(data, toep[g], preferred_element_type=F32)
            upper = made.astype(BF16)
            for k, n in enumerate(blocks):
                conv_hi[lines, n * 128 : (n + 1) * 128] = upper[k * members : (k + 1) * members]
            return carry

        lax.fori_loop(0, 32, one_group, 0, unroll=4)
        top, end = blocks[0] * 128, (blocks[-1] + 1) * 128
        for tile in range(width // 256):
            cols = pl.ds(tile * 256, 256)
            made = lax.dot_general(
                conv_hi[:, top:end], perm[:, cols], flip, preferred_element_type=F32
            )
            made = made + mskip_ref[:, cols] * prod2[128 + top : 128 + end, cols].astype(F32)
            out_ref[top:end, cols] = (
                resid[top:end, cols] + query[top:end, cols] * made
            ).astype(BF16)

    def put(part):
        rows = pl.ds(part * (tokens // 2), tokens // 2)
        return pltpu.make_async_copy(out_ref.at[rows], out_hbm.at[rows], out_sem.at[part])

    products([HALO + 128, HALO + 256, HALO + 384])
    filtered((2, 3))
    put(1).start()
    for make, cond in waits:
        if cond is None:
            copy(*make()).wait_send()
        else:
            pl.when(cond())(lambda make=make: copy(*make()).wait_send())

    @pl.when(ctx > 0)
    def _():
        for k, part in enumerate(tail_parts):
            arrived(tail_in.at[part], sems_of(tail_sem, k), {"ctx": ctx - 1})
        acc[0:HALO, width:] = tail_in[:, width:].astype(F32)
        acc[HALO - 16 : HALO, 0:width] = tail_in[HALO - 16 :, 0:width].astype(F32)

    products([HALO - 128, HALO])
    filtered((0, 1))
    put(0).start()
    put(0).wait()
    put(1).wait()


def local(sizes, *arrays):
    (
        token_ids,
        embedding,
        long_table,
        long_taps,
        long_residue,
        long_rate,
        long_skip,
        medium_gain,
        medium_weight,
        medium_taps,
        medium_group_filter,
        medium_skip,
        filter_group,
    ) = arrays
    ny, nz, nh, nx = sizes
    nch, nctx = nh * nx, 2 * ny * nz
    tokens, width = token_ids.shape[0], embedding.shape[1]
    piece = medium_weight.shape[0]
    hops = max(nz - 1, 1)
    vmem = pl.BlockSpec(memory_space=pltpu.VMEM)
    hbm = pl.BlockSpec(memory_space=pl.ANY)
    dma = pltpu.SemaphoreType.DMA
    return pl.pallas_call(
        functools.partial(kernel, sizes),
        out_shape=jax.ShapeDtypeStruct((tokens, width), BF16),
        in_specs=[vmem, hbm, hbm] + [vmem] * 5 + [hbm] + [vmem] * 4,
        out_specs=hbm,
        scratch_shapes=[
            pltpu.VMEM((tokens, width), BF16),
            pltpu.VMEM((32, width), BF16),
            pltpu.VMEM((3, 32, width), BF16),
            pltpu.VMEM((8, tokens), jnp.int32),
            pltpu.VMEM((nctx * piece, 3 * width), BF16),
            pltpu.VMEM((nch, tokens, width), BF16),
            pltpu.VMEM((HALO + tokens, 3 * width), F32),
            pltpu.VMEM((3, tokens, 32), BF16),
            pltpu.VMEM((8, 128), jnp.int32),
            pltpu.VMEM((width // 128, tokens, 128), F32),
            pltpu.VMEM((tokens, width), F32),
            pltpu.VMEM((tokens, width), F32),
            pltpu.VMEM((width // 128, tokens, 128), F32),
            pltpu.VMEM((32, width), F32),
            pltpu.VMEM((16, 8, width), F32),
            pltpu.VMEM((16, width), F32),
            pltpu.VMEM((16, width), F32),
            pltpu.VMEM((16, width), F32),
            pltpu.VMEM((nz, 16, width), F32),
            pltpu.VMEM((16, width), F32),
            pltpu.VMEM((ny, 16, width), F32),
            pltpu.VMEM((8, tokens), F32),
            pltpu.VMEM((nch, 8, tokens), F32),
            pltpu.VMEM((tokens, 128), F32),
            pltpu.VMEM((tokens, width), BF16),
            pltpu.VMEM((width, width), BF16),
            pltpu.VMEM((32, 256, 128), BF16),
            pltpu.VMEM((HALO, 3 * width), BF16),
            pltpu.VMEM((HALO, 3 * width), BF16),
            pltpu.VMEM((128 + tokens, width), BF16),
            pltpu.VMEM((width, 128 + tokens), BF16),
            pltpu.VMEM((width, tokens), BF16),
            dma((5,)),
            dma((2,)),
            dma((2, hops, 2)),
            dma((2, nz, 4)),
            dma((2, nz, 5)),
            dma((2,)),
            dma((2, nz)),
            dma((2, ny)),
            dma((2, nch)),
            dma((2, 5, 4)),
            dma((2, 4)),
            dma((2, 2)),
            dma((2,)),
        ],
        compiler_params=pltpu.CompilerParams(
            collective_id=0, has_side_effects=True, vmem_limit_bytes=60 << 20
        ),
    )(
        token_ids[None],
        embedding,
        jnp.transpose(long_table, (1, 0, 2)),
        long_taps,
        long_residue.T,
        long_rate.T,
        long_skip[None],
        medium_gain[None],
        jnp.transpose(medium_weight, (1, 0, 2)),
        medium_taps,
        medium_group_filter,
        medium_skip[None],
        filter_group[None],
    )


def solution(mesh, sizes=(4, 4, 2, 4)):
    in_specs = (
        P("ctx"),
        P(None, "ch"),
        P(None, None, "ch"),
        P(None, None, "ch"),
        P("ch", None),
        P("ch", None),
        P("ch"),
        P("ch"),
        P("ctx", None, "ch"),
        P(None, None, "ch"),
        P("ch", None),
        P("ch"),
        P("ch"),
    )
    return jax.shard_map(
        functools.partial(local, sizes),
        mesh=mesh,
        in_specs=in_specs,
        out_specs=P("ctx", "ch"),
        check_vma=False,
    )
```

```python
import functools

import jax
import jax.numpy as jnp
from jax import lax
from jax.experimental import pallas as pl
from jax.experimental.pallas import tpu as pltpu
from jax.sharding import PartitionSpec as P

EPSILON = 1e-06
HALO = 144
F32 = jnp.float32
BF16 = jnp.bfloat16


def kernel(
    sizes,
    token_ref,
    emb_ref,
    table_ref,
    ltaps_ref,
    residue_ref,
    rate_ref,
    lskip_ref,
    gain_ref,
    w_ref,
    mtaps_ref,
    filt_ref,
    mskip_ref,
    group_ref,
    out_hbm,
    out_ref,
    emb,
    table,
    tok_ref,
    weights,
    feats,
    acc,
    hot,
    halo_tok,
    prod,
    query,
    resid,
    conv,
    chan,
    excl,
    end_own,
    end_other,
    chip_own,
    chip_all,
    row_own,
    row_all,
    note_own,
    note_all,
    scale,
    half_norm,
    perm,
    toep,
    tail_out,
    tail_in,
    prod2,
    turned,
    conv_hi,
    load_sem,
    tok_sem,
    z_sem,
    y_sem,
    pair_sem,
    end_sem,
    chip_sem,
    row_sem,
    note_sem,
    x_sem,
    far_sem,
    tail_sem,
    out_sem,
):
    ny, nz, nh, nx = sizes
    nch = nh * nx
    tokens, width = query.shape
    piece = w_ref.shape[1]
    ctx, ch = lax.axis_index("ctx"), lax.axis_index("ch")
    core, chip = ctx % 2, ctx // 2
    z, y = chip % nz, chip // nz
    x, h = ch % nx, ch // nx
    last_ctx = 2 * ny * nz - 1
    waits = []

    def along(yy, zz, cc):
        return {"ctx": (yy * nz + zz) * 2 + cc}

    def across(hh, xx):
        return {"ch": hh * nx + xx}

    def copy(src, dst, sems, to):
        made = pltpu.make_async_remote_copy(
            src_ref=src,
            dst_ref=dst,
            send_sem=sems[0],
            recv_sem=sems[1],
            device_id=to,
            device_id_type=pl.DeviceIdType.MESH,
        )
        return made

    def send(make, cond=None):
        copy(*make()).start()
        waits.append((make, cond))

    def sems_of(ref, *index):
        return ref.at[(0, *index)], ref.at[(1, *index)]

    def arrived(dst, sems, to):
        copy(dst, dst, sems, to).wait_recv()

    barrier = pltpu.get_barrier_semaphore()
    peers = [along(y, z, 1 - core)]
    peers += [along(y, (z + o) % nz, core) for o in range(1, nz)]
    peers += [along((y + o) % ny, z, core) for o in range(1, ny)]
    peers += [{"ch": (ch + o) % nch} for o in range(1, nch)]
    for peer in peers:
        pl.semaphore_signal(barrier, inc=1, device_id=peer, device_id_type=pl.DeviceIdType.MESH)
    has_next = jnp.logical_and(core == 1, ctx < last_ctx)
    has_before = jnp.logical_and(core == 0, ctx > 0)

    @pl.when(has_next)
    def _():
        pl.semaphore_signal(
            barrier, inc=1, device_id={"ctx": ctx + 1}, device_id_type=pl.DeviceIdType.MESH
        )

    @pl.when(has_before)
    def _():
        pl.semaphore_signal(
            barrier, inc=1, device_id={"ctx": ctx - 1}, device_id_type=pl.DeviceIdType.MESH
        )

    def rows_of(slot):
        return pl.ds(pl.multiple_of(slot * piece, piece), piece)

    def part_of(slot, part):
        return pl.ds(pl.multiple_of(slot * piece + part * (piece // 2), piece // 2), piece // 2)

    loads = [
        pltpu.make_async_copy(
            w_ref.at[i], weights.at[rows_of(ctx), pl.ds(i * width, width)], load_sem.at[i]
        )
        for i in range(3)
    ]
    loads.append(pltpu.make_async_copy(emb_ref.at[pl.ds(64, 32)], emb, load_sem.at[3]))
    loads.append(pltpu.make_async_copy(table_ref.at[:, pl.ds(64, 32)], table, load_sem.at[4]))
    for load in loads:
        load.start()
    tok_ref[...] = jnp.broadcast_to(token_ref[...], tok_ref.shape)

    def slot(yy, zz, cc):
        return (yy * nz + zz) * 2 + cc

    def event_of(e):
        if e == 0:
            return z, None
        r = (e - 1) // 2
        if e % 2 == 1:
            return z - 1 - r, lambda: z - 1 - r >= 0
        return z + 1 + r, lambda: z + 1 + r < nz

    def guarded(cond, body):
        if cond is None:
            body()
        else:
            pl.when(cond())(body)

    up, down = (y + 1) % ny, (y + ny - 1) % ny

    def pair(e, kind, rows, cond):
        def make():
            view = weights.at[rows()]
            return view, view, sems_of(pair_sem, event_of(e)[0], kind), along(y, z, 1 - core)

        send(make, cond)

    def y_sends(e, zz, cond):
        if ny > 1:
            for way, to in ((0, up), (1, down)):

                def make(way=way, to=to):
                    view = weights.at[rows_of(slot(y, zz, core))]
                    return view, view, sems_of(y_sem, zz, way), along(to, z, core)

                send(make, cond)

    def z_send(way, hop, zz, cond):
        def inside():
            return z + 1 < nz if way == 0 else z > 0

        def wanted():
            return inside() if cond is None else jnp.logical_and(cond(), inside())

        def make():
            view = weights.at[rows_of(slot(y, zz, core))]
            to = z + 1 if way == 0 else z - 1
            return view, view, sems_of(z_sem, hop, way), along(y, to, core)

        pl.when(inside())(lambda: send(make, wanted))

    def own_weights():
        if nz > 1:
            z_send(0, 0, z, None)
            z_send(1, 0, z, None)
        y_sends(0, z, None)
        pair(0, 0, lambda: rows_of(slot(y, z, core)), None)

    def z_forward(r):
        for way in (0, 1):
            e = 1 + 2 * r + way
            zz, valid = event_of(e)

            def body(way=way, e=e, zz=zz, valid=valid):
                rows = rows_of(slot(y, zz, core))
                arrived(
                    weights.at[rows],
                    (z_sem.at[0, r, way], z_sem.at[1, r, way]),
                    along(y, zz, core),
                )
                if r + 1 < nz - 1:
                    z_send(way, r + 1, zz, valid)

            guarded(valid, body)

    def z_spread(r):
        for way in (0, 1):
            e = 1 + 2 * r + way
            zz, valid = event_of(e)

            def body(e=e, zz=zz, valid=valid):
                y_sends(e, zz, valid)
                pair(e, 0, lambda: rows_of(slot(y, zz, core)), valid)

            guarded(valid, body)

    def z_round(r):
        z_forward(r)
        z_spread(r)

    def y_first(e):
        zz, valid = event_of(e)

        def body():
            for way, origin, to in ((0, down, up), (1, up, down)):
                rows = rows_of(slot(origin, zz, core))
                arrived(
                    weights.at[rows],
                    sems_of(y_sem, zz, way),
                    along(origin, z, core),
                )

                def make(way=way, origin=origin, to=to):
                    view = weights.at[part_of(slot(origin, zz, core), way)]
                    return view, view, sems_of(y_sem, zz, 2 + way), along(to, z, core)

                send(make, valid)
                pair(e, 1 + way, lambda origin=origin: rows_of(slot(origin, zz, core)), valid)

        if ny > 1:
            guarded(valid, body)

    def y_second(e):
        zz, valid = event_of(e)

        def body():
            for way, origin in ((0, down), (1, up)):
                half = part_of(slot((y + 2) % ny, zz, core), way)
                arrived(
                    weights.at[half],
                    sems_of(y_sem, zz, 2 + way),
                    along(origin, z, core),
                )
                pair(
                    e, 3 + way, lambda way=way: part_of(slot((y + 2) % ny, zz, core), way), valid
                )

        if ny > 1:
            guarded(valid, body)

    def pair_in(e, kinds):
        zz, valid = event_of(e)

        def body():
            other = along(y, z, 1 - core)

            def one(kind, rows):
                if kind in kinds:
                    arrived(weights.at[rows], sems_of(pair_sem, zz, kind), other)

            one(0, rows_of(slot(y, zz, 1 - core)))
            if ny > 1:
                one(1, rows_of(slot(down, zz, 1 - core)))
                one(2, rows_of(slot(up, zz, 1 - core)))
                one(3, part_of(slot((y + 2) % ny, zz, 1 - core), 0))
                one(4, part_of(slot((y + 2) % ny, zz, 1 - core), 1))

        guarded(valid, body)

    events = list(range(1 + 2 * (nz - 1)))

    group_row = (group_ref[...] - ch * (width // 16)).astype(F32)
    of_group = (
        lax.broadcasted_iota(jnp.int32, (32, width), 0).astype(F32) == group_row
    ).astype(F32)
    rate_in = rate_ref[...]
    twice = 2.0 * rate_in
    series = jnp.ones_like(twice)
    for k in range(9, 1, -1):
        series = 1.0 - twice * (1.0 / k) * series
    both = jnp.concatenate([rate_in, residue_ref[...] * jnp.sqrt(twice * series)], axis=0)
    chan[...] = jnp.dot(
        both, of_group, precision=lax.Precision.HIGHEST, preferred_element_type=F32
    )

    def one_hots(joined, count):
        codes = 64 + lax.broadcasted_iota(jnp.int32, (32, count), 0)
        for back in range(3):
            shifted = joined if back == 0 else pltpu.roll(joined, back, 1)
            row = shifted[0:1, 128:]
            hot[back, 0:count] = (row == codes).astype(F32).T.astype(BF16)

    def streams(rows):
        for tile in range(width // 128):
            cols = pl.ds(tile * 128, 128)

            def mixed(i, cols=cols):
                total = None
                for back in range(3):
                    picked = jnp.dot(
                        hot[back, 0:rows], table[i, :, cols], preferred_element_type=F32
                    )
                    term = ltaps_ref[back, i : i + 1, cols] * picked
                    total = term if total is None else total + term
                return total

            key = mixed(1)
            prod[tile, 0:rows] = (key * mixed(2)).astype(BF16).astype(F32)
            query[0:rows, cols] = mixed(0)

    one_hots(jnp.concatenate([jnp.full((8, 128), -1, jnp.int32), tok_ref[...]], axis=1), tokens)
    loads[3].wait()
    loads[4].wait()
    resid[...] = jnp.dot(hot[0], emb[...], preferred_element_type=F32)
    streams(tokens)

    extra = jnp.logical_or(has_next, has_before)
    pl.semaphore_wait(barrier, len(peers) + extra.astype(jnp.int32))
    tail_tok = pl.ds(tokens - 128, 128)

    @pl.when(ctx < last_ctx)
    def _():
        send(
            lambda: (tok_ref.at[:, tail_tok], halo_tok, sems_of(tok_sem), {"ctx": ctx + 1}),
            lambda: ctx < last_ctx,
        )

    for load in loads[:3]:
        load.wait()
    own_weights()

    taps = filt_ref.shape[1]

    def make_toep(g, carry):
        line = filt_ref[pl.ds(g, 1), :]
        line = jnp.concatenate([line, jnp.zeros((1, taps), F32)], axis=1)
        spread = jnp.broadcast_to(line, (2 * taps, 2 * taps))
        turned_line = pltpu.roll(spread, taps, 1, stride=1, stride_axis=0)
        toep[g] = turned_line[:, :taps].astype(BF16)
        return carry

    lax.fori_loop(0, filt_ref.shape[0], make_toep, 0)
    lanes = lax.broadcasted_iota(jnp.int32, (128, width), 1)
    rank = jnp.zeros((1, width), F32)
    group_col = jnp.broadcast_to(group_row, (128, width)).T
    for tile in range(width // 128):
        mine = group_col[tile * 128 : (tile + 1) * 128, 0:1]
        above = tile * 128 + lax.broadcasted_iota(jnp.int32, (128, width), 0) < lanes
        same = jnp.logical_and(mine == group_row, above)
        rank = rank + jnp.sum(same.astype(F32), axis=0, keepdims=True)
    placed = group_row * float(width // 32) + rank
    for tile in range(width // 128):
        place = (tile * 128 + lax.broadcasted_iota(jnp.int32, (128, width), 0)).astype(F32)
        perm[tile * 128 : (tile + 1) * 128, :] = (place == placed).astype(F32).astype(BF16)

    @pl.when(ctx > 0)
    def _():
        arrived(halo_tok, (tok_sem.at[0], tok_sem.at[1]), {"ctx": ctx - 1})
        one_hots(jnp.concatenate([halo_tok[...], tok_ref[:, 0:128]], axis=1), 128)
        streams(16)

    chunk = tokens // 8
    chunk_id = lax.broadcasted_iota(jnp.int32, (8, 128), 0)

    def row_b(ref, p, cols):
        return jnp.broadcast_to(ref[p : p + 1, cols], (8, 128))

    for tile in range(width // 128):
        cols = pl.ds(tile * 128, 128)
        decay = [jnp.exp(-row_b(chan, p, cols)) for p in range(16)]

        def step(k, states, tile=tile, decay=decay):
            row = prod[tile, pl.ds(k, 8, stride=chunk), :]
            return tuple(d * s + row for d, s in zip(decay, states))

        states = lax.fori_loop(
            0, chunk, step, tuple(jnp.zeros((8, 128), F32) for _ in range(16)), unroll=4
        )
        for p in range(16):
            rate = row_b(chan, p, cols) * float(chunk)
            total = states[p]
            for by in (1, 2, 4):
                moved = jnp.exp(-rate * float(by)) * pltpu.roll(total, by, 0)
                total = total + jnp.where(chunk_id >= by, moved, 0.0)
            end_own[p : p + 1, cols] = total[7:8]
            excl[p, :, cols] = jnp.where(chunk_id >= 1, pltpu.roll(total, 1, 0), 0.0)

    def own_conv(tiles):
        for tile in tiles:
            cols = pl.ds(tile * 128, 128)
            decay = [jnp.exp(-row_b(chan, p, cols)) for p in range(16)]
            weigh = [row_b(chan, 16 + p, cols) for p in range(16)]

            def step2(k, states, tile=tile, decay=decay, weigh=weigh):
                where = pl.ds(k, 8, stride=chunk)
                row = prod[tile, where, :]
                states = tuple(d * s + row for d, s in zip(decay, states))
                sums = [None] * 4
                for p in range(16):
                    term = weigh[p] * states[p]
                    sums[p % 4] = term if sums[p % 4] is None else sums[p % 4] + term
                conv[tile, where, :] = (sums[0] + sums[1]) + (sums[2] + sums[3])
                return states

            start = tuple(excl[p, :, cols] for p in range(16))
            lax.fori_loop(0, chunk, step2, start, unroll=2)

    rates = chan[0:16, :]
    send(lambda: (end_own, end_other, sems_of(end_sem), along(y, z, 1 - core)))
    arrived(end_other, (end_sem.at[0], end_sem.at[1]), along(y, z, 1 - core))
    first = jnp.where(core == 0, end_own[...], end_other[...])
    second = jnp.where(core == 0, end_other[...], end_own[...])
    decay_dev = jnp.exp(-rates * float(tokens))
    chip_own[...] = first * decay_dev + second
    for o in range(1, nz):
        send(
            lambda o=o: (
                chip_own,
                chip_all.at[z],
                (chip_sem.at[0, (z + o) % nz], chip_sem.at[1, z]),
                along(y, (z + o) % nz, core),
            )
        )
    own_conv((0, 1))
    if nz > 1:
        z_forward(0)
    for o in range(1, nz):
        origin = (z + nz - o) % nz
        arrived(
            chip_all.at[origin], (chip_sem.at[0, z], chip_sem.at[1, origin]), along(y, origin, core)
        )
    decay_chip = jnp.exp(-rates * float(2 * tokens))
    whole = None
    for zz in range(nz):
        if nz == 1:
            this = chip_own[...]
        else:
            this = jnp.where(z == zz, chip_own[...], chip_all[zz])
        whole = this if whole is None else whole * decay_chip + this
    row_own[...] = whole
    for o in range(1, ny):

        @pl.when(y + o < ny)
        def _(o=o):
            send(
                lambda: (
                    row_own,
                    row_all.at[y],
                    (row_sem.at[0, (y + o) % ny], row_sem.at[1, y]),
                    along((y + o) % ny, z, core),
                ),
                lambda: y + o < ny,
            )

    if nz > 1:
        z_spread(0)
    y_first(0)
    own_conv((2, 3))
    for o in range(1, ny):

        @pl.when(y >= o)
        def _(o=o):
            origin = (y + ny - o) % ny
            arrived(
                row_all.at[origin],
                (row_sem.at[0, y], row_sem.at[1, origin]),
                along(origin, z, core),
            )

    decay_row = jnp.exp(-rates * float(2 * tokens * nz))
    carried = jnp.zeros((16, width), F32)
    for yy in range(ny - 1):
        carried = jnp.where(yy < y, carried * decay_row + row_all[yy], carried)
    for zz in range(nz - 1):
        carried = jnp.where(zz < z, carried * decay_chip + chip_all[zz], carried)
    carried = jnp.where(core == 1, carried * decay_dev + first, carried)
    end_other[...] = carried

    for tile in range(width // 128):
        cols = pl.ds(tile * 128, 128)
        start = []
        for p in range(16):
            rate = row_b(chan, p, cols)
            since = rate * (chunk_id * chunk + 1).astype(F32)
            start.append(row_b(chan, 16 + p, cols) * row_b(end_other, p, cols) * jnp.exp(-since))
        decay = [jnp.exp(-row_b(chan, p, cols)) for p in range(16)]

        def step3(k, states, tile=tile, decay=decay):
            where = pl.ds(k, 8, stride=chunk)
            sums = list(states[:4])
            for p in range(4, 16):
                sums[p % 4] = sums[p % 4] + states[p]
            conv[tile, where, :] += (sums[0] + sums[1]) + (sums[2] + sums[3])
            return tuple(d * s for d, s in zip(decay, states))

        lax.fori_loop(0, chunk, step3, tuple(start), unroll=4)

    squares = None
    for tile in range(width // 128):
        cols = pl.ds(tile * 128, 128)
        whole = conv[tile] + lskip_ref[:, cols] * prod[tile]
        middle = (resid[:, cols] + query[:, cols] * whole).astype(BF16)
        feats[ch, :, cols] = middle
        wide = middle.astype(F32)
        resid[:, cols] = wide
        squares = wide * wide if squares is None else squares + wide * wide
    note_own[...] = jnp.broadcast_to(jnp.sum(squares.T, axis=0, keepdims=True), note_own.shape)
    note_own[1:2, :] = gain_ref[...].astype(F32)
    for o in range(1, nch):
        send(
            lambda o=o: (
                note_own,
                note_all.at[ch],
                (note_sem.at[0, (ch + o) % nch], note_sem.at[1, ch]),
                {"ch": (ch + o) % nch},
            )
        )

    right, left = (x + 1) % nx, (x + nx - 1) % nx
    far_parts = 4
    far_rows = tokens // far_parts

    def rows_x(e):
        return (0, tokens) if e == 0 else ((e - 1) * far_rows, far_rows)

    def half_x(e, way):
        base, count = rows_x(e)
        return pl.ds(base + way * (count // 2), count // 2)

    def x_sends(e):
        if nx > 1:
            for way, to in ((0, right), (1, left)):

                def make(way=way, to=to):
                    view = feats.at[side(e) * nx + x, pl.ds(*rows_x(e))]
                    return view, view, sems_of(x_sem, e, way), across(h, to)

                send(make)

    def side(e):
        return h if e == 0 else 1 - h

    def x_first(e):
        if nx > 1:
            for way, origin, to in ((0, left, right), (1, right, left)):
                block = side(e) * nx + origin
                arrived(
                    feats.at[block, pl.ds(*rows_x(e))], sems_of(x_sem, e, way), across(h, origin)
                )

                def make(way=way, block=block, to=to):
                    part = feats.at[block, half_x(e, way)]
                    return part, part, sems_of(x_sem, e, 2 + way), across(h, to)

                send(make)

    def x_second(e):
        if nx > 1:
            for way, origin in ((0, left), (1, right)):
                part = feats.at[side(e) * nx + (x + 2) % nx, half_x(e, way)]
                arrived(part, sems_of(x_sem, e, 2 + way), across(h, origin))

    def far_in(k):
        if nh > 1:
            part = feats.at[(1 - h) * nx + x, pl.ds(k * far_rows, far_rows)]
            arrived(part, sems_of(far_sem, k), across(1 - h, x))
            x_sends(1 + k)

    def x_far_first(k):
        if nh > 1:
            x_first(1 + k)

    x_sends(0)
    def far_out(*which):
        if nh > 1:
            for k in which:

                def make(k=k):
                    part = feats.at[ch, pl.ds(k * far_rows, far_rows)]
                    return part, part, sems_of(far_sem, k), across(1 - h, x)

                send(make)

    if nz > 2:
        z_round(1)

    def y_first_if(*which):
        for e in which:
            if e in events:
                y_first(e)

    def y_second_if(*which):
        for e in which:
            if e in events:
                y_second(e)

    acc[...] = jnp.zeros_like(acc)
    y_first_if(1)
    x_first(0)
    if nz > 3:
        z_round(2)
    far_out(*range(far_parts))
    y_first_if(2)
    far_in(0)
    y_first_if(3, 4)
    far_in(1)
    x_far_first(0)
    y_second(0)
    far_in(2)
    x_far_first(1)
    y_first_if(5, 6)
    far_in(3)

    for o in range(1, nch):
        origin = (ch + nch - o) % nch
        arrived(
            note_all.at[origin], (note_sem.at[0, ch], note_sem.at[1, origin]), {"ch": origin}
        )
    note_all[ch] = note_own[...]
    total = note_all[0, 0:1, :]
    for o in range(1, nch):
        total = total + note_all[o, 0:1, :]
    factor = lax.rsqrt(total / float(width * nch) + EPSILON)
    scale[...] = jnp.broadcast_to(factor, (128, tokens)).T

    per_tile = 256
    per_row = nch // ny
    wide_all = acc.shape[1]

    def block_product(block, top, count):
        gain = note_all[block, 1:2, :]
        for tile in range(width // 128):
            cols = pl.ds(tile * 128, 128)
            wide = feats[block, top : top + count, cols].astype(F32) * scale[top : top + count, :]
            half_norm[top : top + count, cols] = (
                wide * gain[:, tile * 128 : (tile + 1) * 128]
            ).astype(BF16)
        rows = pl.ds(pl.multiple_of(block * width, width), width)
        for tile in range(wide_all // per_tile):
            cols = pl.ds(tile * per_tile, per_tile)
            acc[HALO + top : HALO + top + count, cols] += jnp.dot(
                half_norm[top : top + count, :], weights[rows, cols], preferred_element_type=F32
            )

    def early(block):
        same = block // nx == h
        if ny == 1:
            return same
        return jnp.logical_and(same, block // per_row != (y + 2) % ny)

    def late(block):
        return jnp.logical_not(early(block))

    def product_if(wanted, first, count, top, rows):
        def body(i, carry):
            block = first + i
            if wanted is None:
                block_product(block, top, rows)
            else:
                pl.when(wanted(block))(lambda: block_product(block, top, rows))
            return carry

        lax.fori_loop(0, count, body, 0)

    split = nch > 1
    x_second(0)
    x_far_first(2)
    y_second_if(1, 2, 3, 4)
    for e in events:
        pair_in(e, (0, 1, 2))
    x_far_first(3)
    y_second_if(5, 6)
    if split:
        product_if(early, h * nx, nx, 0, tokens)
    for e in events:
        pair_in(e, (3, 4))
    if split:
        product_if(late, h * nx, nx, 0, tokens)
    if nh > 1:
        for k in range(far_parts):
            x_second(1 + k)

    body_rows = tokens - HALO
    if split:
        product_if(None, (1 - h) * nx, nx, body_rows, HALO)
    else:
        block_product(0, body_rows, HALO)
    for tile in range(wide_all // 256):
        cols = pl.ds(tile * 256, 256)
        last = acc[tokens:, cols].astype(BF16)
        tail_out[:, cols] = last
        acc[tokens:, cols] = last.astype(F32)
    tail_parts = (
        (pl.ds(0, HALO), pl.ds(width, 2 * width)),
        (pl.ds(HALO - 16, 16), pl.ds(0, width)),
    )

    @pl.when(ctx < last_ctx)
    def _():
        for k, part in enumerate(tail_parts):
            send(
                lambda k=k, part=part: (
                    tail_out.at[part],
                    tail_in.at[part],
                    sems_of(tail_sem, k),
                    {"ctx": ctx + 1},
                ),
                lambda: ctx < last_ctx,
            )

    if split:
        product_if(None, (1 - h) * nx, nx, 0, body_rows)
    else:
        block_product(0, 0, body_rows)
    for tile in range(wide_all // 256):
        cols = pl.ds(tile * 256, 256)
        acc[HALO:tokens, cols] = acc[HALO:tokens, cols].astype(BF16).astype(F32)

    def mixed2(i, base, count, tile):
        cols = pl.ds(i * width + tile * 128, 128)
        at = pl.ds(tile * 128, 128)
        total = None
        for back in range(3):
            term = (
                mtaps_ref[back, i : i + 1, at]
                * acc[base - back : base - back + count, cols]
            )
            total = term if total is None else total + term
        return total

    members = width // 32
    flip = (((0,), (0,)), ((), ()))

    def products(bases):
        for tile in range(width // 128):
            cols = pl.ds(tile * 128, 128)
            for base in bases:
                made = mixed2(1, base, 128, tile) * mixed2(2, base, 128, tile)
                prod2[base - HALO + 128 : base - HALO + 256, cols] = made.astype(BF16)
                if base >= HALO:
                    query[base - HALO : base - HALO + 128, cols] = mixed2(0, base, 128, tile)
        top, end = bases[0] - HALO + 128, bases[-1] - HALO + 256
        for tile in range(width // 128):
            lines = pl.ds(tile * 128, 128)
            made = lax.dot_general(
                perm[lines, :],
                prod2[top:end, :],
                (((1,), (1,)), ((), ())),
                preferred_element_type=F32,
            )
            turned[lines, top:end] = made.astype(BF16)

    def filtered(blocks):
        def one_group(g, carry):
            lines = pl.ds(pl.multiple_of(g * members, members), members)
            data = jnp.concatenate(
                [turned[lines, n * 128 : n * 128 + 256] for n in blocks], axis=0
            )
            made = jnp.dot(data, toep[g], preferred_element_type=F32)
            upper = made.astype(BF16)
            for k, n in enumerate(blocks):
                conv_hi[lines, n * 128 : (n + 1) * 128] = upper[k * members : (k + 1) * members]
            return carry

        lax.fori_loop(0, 32, one_group, 0, unroll=4)
        top, end = blocks[0] * 128, (blocks[-1] + 1) * 128
        for tile in range(width // 256):
            cols = pl.ds(tile * 256, 256)
            made = lax.dot_general(
                conv_hi[:, top:end], perm[:, cols], flip, preferred_element_type=F32
            )
            made = made + mskip_ref[:, cols] * prod2[128 + top : 128 + end, cols].astype(F32)
            out_ref[top:end, cols] = (
                resid[top:end, cols] + query[top:end, cols] * made
            ).astype(BF16)

    def put(part):
        rows = pl.ds(part * (tokens // 2), tokens // 2)
        return pltpu.make_async_copy(out_ref.at[rows], out_hbm.at[rows], out_sem.at[part])

    products([HALO + 128, HALO + 256, HALO + 384])
    filtered((2, 3))
    put(1).start()
    for make, cond in waits:
        if cond is None:
            copy(*make()).wait_send()
        else:
            pl.when(cond())(lambda make=make: copy(*make()).wait_send())

    @pl.when(ctx > 0)
    def _():
        for k, part in enumerate(tail_parts):
            arrived(tail_in.at[part], sems_of(tail_sem, k), {"ctx": ctx - 1})
        acc[0:HALO, width:] = tail_in[:, width:].astype(F32)
        acc[HALO - 16 : HALO, 0:width] = tail_in[HALO - 16 :, 0:width].astype(F32)

    products([HALO - 128, HALO])
    filtered((0, 1))
    put(0).start()
    put(0).wait()
    put(1).wait()


def local(sizes, *arrays):
    (
        token_ids,
        embedding,
        long_table,
        long_taps,
        long_residue,
        long_rate,
        long_skip,
        medium_gain,
        medium_weight,
        medium_taps,
        medium_group_filter,
        medium_skip,
        filter_group,
    ) = arrays
    ny, nz, nh, nx = sizes
    nch, nctx = nh * nx, 2 * ny * nz
    tokens, width = token_ids.shape[0], embedding.shape[1]
    piece = medium_weight.shape[0]
    hops = max(nz - 1, 1)
    vmem = pl.BlockSpec(memory_space=pltpu.VMEM)
    hbm = pl.BlockSpec(memory_space=pl.ANY)
    dma = pltpu.SemaphoreType.DMA
    return pl.pallas_call(
        functools.partial(kernel, sizes),
        out_shape=jax.ShapeDtypeStruct((tokens, width), BF16),
        in_specs=[vmem, hbm, hbm] + [vmem] * 5 + [hbm] + [vmem] * 4,
        out_specs=hbm,
        scratch_shapes=[
            pltpu.VMEM((tokens, width), BF16),
            pltpu.VMEM((32, width), BF16),
            pltpu.VMEM((3, 32, width), BF16),
            pltpu.VMEM((8, tokens), jnp.int32),
            pltpu.VMEM((nctx * piece, 3 * width), BF16),
            pltpu.VMEM((nch, tokens, width), BF16),
            pltpu.VMEM((HALO + tokens, 3 * width), F32),
            pltpu.VMEM((3, tokens, 32), BF16),
            pltpu.VMEM((8, 128), jnp.int32),
            pltpu.VMEM((width // 128, tokens, 128), F32),
            pltpu.VMEM((tokens, width), F32),
            pltpu.VMEM((tokens, width), F32),
            pltpu.VMEM((width // 128, tokens, 128), F32),
            pltpu.VMEM((32, width), F32),
            pltpu.VMEM((16, 8, width), F32),
            pltpu.VMEM((16, width), F32),
            pltpu.VMEM((16, width), F32),
            pltpu.VMEM((16, width), F32),
            pltpu.VMEM((nz, 16, width), F32),
            pltpu.VMEM((16, width), F32),
            pltpu.VMEM((ny, 16, width), F32),
            pltpu.VMEM((8, tokens), F32),
            pltpu.VMEM((nch, 8, tokens), F32),
            pltpu.VMEM((tokens, 128), F32),
            pltpu.VMEM((tokens, width), BF16),
            pltpu.VMEM((width, width), BF16),
            pltpu.VMEM((32, 256, 128), BF16),
            pltpu.VMEM((HALO, 3 * width), BF16),
            pltpu.VMEM((HALO, 3 * width), BF16),
            pltpu.VMEM((128 + tokens, width), BF16),
            pltpu.VMEM((width, 128 + tokens), BF16),
            pltpu.VMEM((width, tokens), BF16),
            dma((5,)),
            dma((2,)),
            dma((2, hops, 2)),
            dma((2, nz, 4)),
            dma((2, nz, 5)),
            dma((2,)),
            dma((2, nz)),
            dma((2, ny)),
            dma((2, nch)),
            dma((2, 5, 4)),
            dma((2, 4)),
            dma((2, 2)),
            dma((2,)),
        ],
        compiler_params=pltpu.CompilerParams(
            collective_id=0, has_side_effects=True, vmem_limit_bytes=60 << 20
        ),
    )(
        token_ids[None],
        embedding,
        jnp.transpose(long_table, (1, 0, 2)),
        long_taps,
        long_residue.T,
        long_rate.T,
        long_skip[None],
        medium_gain[None],
        jnp.transpose(medium_weight, (1, 0, 2)),
        medium_taps,
        medium_group_filter,
        medium_skip[None],
        filter_group[None],
    )


def solution(mesh, sizes=(4, 4, 2, 4)):
    in_specs = (
        P("ctx"),
        P(None, "ch"),
        P(None, None, "ch"),
        P(None, None, "ch"),
        P("ch", None),
        P("ch", None),
        P("ch"),
        P("ch"),
        P("ctx", None, "ch"),
        P(None, None, "ch"),
        P("ch", None),
        P("ch"),
        P("ch"),
    )
    return jax.shard_map(
        functools.partial(local, sizes),
        mesh=mesh,
        in_specs=in_specs,
        out_specs=P("ctx", "ch"),
        check_vma=False,
    )
```
